32 devices in a mesh: win: 2 (over y), vel: 8 (over z, x), sp: 2 (over core).
Axes of the slice: x: 2, y: 2, z: 4, core: 2. Of those that a mesh axis runs over, the one named last changes fastest.
Arguments:
- f_start: float32 [2, 1536, 64, 128], P('win', 'vel', 'sp'), may hold values from 0 to 15, as said below
- relax_rate: float32 [64, 128], P('sp'), may hold values from 0.1 to 10
Outputs:
- corrected: float32 [2, 4, 64, 128], P('win', None, 'sp')
- lifted: float32 [2, 1536, 64, 128], P('win', 'vel', 'sp')
The draws below stay inside these ranges and needn't reach their ends.
Inputs may be any that keep to these rules, and one draw needn't show every extreme that they name: `f_start`: no entry is negative.
All inputs are finite; a program needn't handle non-finite values.
Results may differ from the reference program's by a relative error of at most 0.00021.
Values sent between devices are 32-bit elements; how exact they have to be, the bound alone decides.
A program may use at most 64 MiB of HBM per device.

```python
import math
import jax
import jax.numpy as jnp
from jax import lax

NVX = 48
NVY = 32
NX = 64
NY = 128
NV = 1536
WINDOWS = 2


def draw_f_start(key, part):
    random_seeds = jax.random.split(key, 5)
    grid_volume = (WINDOWS, 1, NX, NY)
    mass_per_volume = jnp.exp(jax.random.uniform(random_seeds[0], grid_volume, jnp.float32, math.log(0.2), math.log(2.0)))
    pointwise_thermal_level = jnp.exp(jax.random.uniform(random_seeds[1], grid_volume, jnp.float32, math.log(0.2), math.log(1.5)))
    horizontal_flow = jax.random.uniform(random_seeds[2], grid_volume, jnp.float32, -0.5, 0.5)
    upward_flow = jax.random.uniform(random_seeds[3], grid_volume, jnp.float32, -0.5, 0.5)
    full = (WINDOWS, NV, NX, NY)
    noise = jnp.clip(0.15 * jax.random.normal(random_seeds[4], full, jnp.float32), -0.45, 0.45)
    index = jnp.arange(NV, dtype=jnp.int32)
    vel_x = -6.0 + ((index // NVY).astype(jnp.float32) + 0.5) * (12.0 / NVX)
    vel_y = -6.0 + ((index % NVY).astype(jnp.float32) + 0.5) * (12.0 / NVY)
    horizontal_gradient = vel_x[None, :, None, None] - horizontal_flow
    upward_gradient = vel_y[None, :, None, None] - upward_flow
    gaussian_profile = mass_per_volume / pointwise_thermal_level * jnp.exp(-(horizontal_gradient * horizontal_gradient + upward_gradient * upward_gradient) / (2.0 * pointwise_thermal_level))
    return (gaussian_profile * (1.0 + noise)).astype(jnp.float32)


def block_levels(key, extent, cuts, low, top_value):
    loudness, own = 1.0, jax.random.fold_in(key, 6)
    for axis_at, shards_of in cuts:
        heights = jnp.exp(jax.random.uniform(jax.random.fold_in(own, axis_at), (shards_of,), jnp.float32, low / len(cuts), top_value / len(cuts)))
        loudness = loudness * jnp.repeat(heights, extent[axis_at] // shards_of).reshape([-1 if axis == axis_at else 1 for axis in range(len(extent))])
    return loudness


def setup_inputs(seed: int = 0) -> dict:
    keys = jax.random.split(jax.random.key(seed), 3)
    f_start = draw_f_start(jax.random.fold_in(keys[2], 71), 0)
    relax_rate = jnp.clip(jnp.exp(math.log(10.0) - 4.6051702 * jax.random.uniform(keys[1], (NX, NY), jnp.float32) ** block_levels(keys[1], (NX, NY), ((0, 2),), -0.2, 0.2)), 0.1, 10.0)
    return dict(f_start=f_start, relax_rate=relax_rate)


vel_max = 6.0
fine_ratio = 0.075
coarse_ratio = 0.15
density_floor = 0.3
thermal_lower_bound = 0.3

def velocity_table(first, count):
    index = first + jnp.arange(count, dtype=jnp.int32)
    vel_x = -vel_max + ((index // NVY).astype(jnp.float32) + 0.5) * (2.0 * vel_max / NVX)
    vel_y = -vel_max + ((index % NVY).astype(jnp.float32) + 0.5) * (2.0 * vel_max / NVY)
    return (vel_x, vel_y)

def moment_table(vel_x, vel_y):
    weight_unit = 2.0 * vel_max / NVX * (2.0 * vel_max / NVY) / (2.0 * math.pi)
    return jnp.stack([jnp.ones_like(vel_x), vel_x, vel_y, 0.5 * (vel_x * vel_x + vel_y * vel_y)]) * weight_unit

def moments(field, table):
    flat = field.reshape(field.shape[0], -1)
    out = jnp.dot(table, flat, precision=lax.Precision.HIGHEST, preferred_element_type=jnp.float32)
    return out.reshape(4, field.shape[1], field.shape[2])

def physical_variables(distribution_array):
    mass_per_volume = jnp.maximum(distribution_array[0], density_floor)
    horizontal_flow = distribution_array[1] / mass_per_volume
    upward_flow = distribution_array[2] / mass_per_volume
    inner_volumes = (distribution_array[3] - 0.5 * (distribution_array[1] * horizontal_flow + distribution_array[2] * upward_flow)) / mass_per_volume
    pointwise_thermal_level = jnp.maximum(inner_volumes, thermal_lower_bound)
    return (mass_per_volume, horizontal_flow, upward_flow, pointwise_thermal_level)

def equilibrium_density(distribution_array, vel_x, vel_y):
    mass_per_volume, horizontal_flow, upward_flow, pointwise_thermal_level = physical_variables(distribution_array)
    horizontal_gradient = vel_x[:, None, None] - horizontal_flow[None]
    upward_gradient = vel_y[:, None, None] - upward_flow[None]
    return (mass_per_volume / pointwise_thermal_level)[None] * jnp.exp(-(horizontal_gradient * horizontal_gradient + upward_gradient * upward_gradient) / (2.0 * pointwise_thermal_level[None]))

def transport(field, left, right, vel_x, vel_y):
    coef_x = (vel_x * fine_ratio)[:, None, None]
    coef_y = (vel_y * fine_ratio)[:, None, None]
    below = jnp.roll(field, 1, axis=2)
    above = jnp.roll(field, -1, axis=2)
    out = field - jnp.maximum(coef_x, 0.0) * (field - left) - jnp.minimum(coef_x, 0.0) * (right - field)
    return out - jnp.maximum(coef_y, 0.0) * (field - below) - jnp.minimum(coef_y, 0.0) * (above - field)

def euler_update(padded_array):
    mass_per_volume, horizontal_flow, upward_flow, pointwise_thermal_level = physical_variables(padded_array)
    normal_stress = mass_per_volume * pointwise_thermal_level
    acoustic_wave_rate = jnp.sqrt(2.0 * pointwise_thermal_level)
    flux_x = jnp.stack([padded_array[1], padded_array[1] * horizontal_flow + normal_stress, padded_array[2] * horizontal_flow, (padded_array[3] + normal_stress) * horizontal_flow])
    flux_y = jnp.stack([padded_array[2], padded_array[1] * upward_flow, padded_array[2] * upward_flow + normal_stress, (padded_array[3] + normal_stress) * upward_flow])
    reach_x = jnp.abs(horizontal_flow) + acoustic_wave_rate
    reach_y = jnp.abs(upward_flow) + acoustic_wave_rate
    face_x = 0.5 * (flux_x[:, :-1, 1:-1] + flux_x[:, 1:, 1:-1]) - 0.5 * jnp.maximum(reach_x[:-1, 1:-1], reach_x[1:, 1:-1])[None] * (padded_array[:, 1:, 1:-1] - padded_array[:, :-1, 1:-1])
    face_y = 0.5 * (flux_y[:, 1:-1, :-1] + flux_y[:, 1:-1, 1:]) - 0.5 * jnp.maximum(reach_y[1:-1, :-1], reach_y[1:-1, 1:])[None] * (padded_array[:, 1:-1, 1:] - padded_array[:, 1:-1, :-1])
    return padded_array[:, 1:-1, 1:-1] - coarse_ratio * (face_x[:, 1:] - face_x[:, :-1] + (face_y[:, :, 1:] - face_y[:, :, :-1]))

def coarse(distribution_array):
    return euler_update(jnp.pad(distribution_array, ((0, 0), (1, 1), (1, 1)), mode='wrap'))

def fine(field, rates, vel_x, vel_y, table):
    start = moments(field, table)
    current = field
    for step in range(2):
        star = transport(current, jnp.roll(current, 1, axis=1), jnp.roll(current, -1, axis=1), vel_x, vel_y)
        distribution_array = moments(star, table)
        current = (star + rates[None] * equilibrium_density(distribution_array, vel_x, vel_y)) / (1.0 + rates[None])
    return (start, distribution_array, current)

def reference(f_start, relax_rate):
    vel_x, vel_y = velocity_table(0, NV)
    table = moment_table(vel_x, vel_y)

    def first_pass(field):
        start, ending, unused = fine(field, relax_rate, vel_x, vel_y, table)
        return (start, ending)
    starts, endings = lax.map(first_pass, f_start)
    delta = endings - lax.map(coarse, starts)
    distribution_array = starts[0]
    outs = []
    for time_window in range(WINDOWS):
        distribution_array = coarse(distribution_array) + delta[time_window]
        outs.append(distribution_array)
    corrected = jnp.stack(outs)

    def lift(items):
        field, target, ending = items
        unused_a, unused_b, current = fine(field, relax_rate, vel_x, vel_y, table)
        return current + equilibrium_density(target, vel_x, vel_y) - equilibrium_density(ending, vel_x, vel_y)
    lifted = lax.map(lift, (f_start, corrected, endings))
    return (corrected, lifted)
```

```python
import functools
import math

import jax
import jax.numpy as jnp
from jax import lax
from jax.experimental import pallas as pl
from jax.experimental.pallas import tpu as pltpu
from jax.sharding import PartitionSpec as P

NVX = 48
NVY = 32
HALF = NVY // 2
TILE = 8
vel_max = 6.0
fine_ratio = 0.075
coarse_ratio = 0.15
density_floor = 0.3
thermal_lower_bound = 0.3
DVX = 2.0 * vel_max / NVX
DVY = 2.0 * vel_max / NVY
WEIGHT = DVX * DVY / (2.0 * math.pi)
MESH = pl.DeviceIdType.MESH
f32 = jnp.float32


def physical_variables(u):
    rs = jnp.maximum(u[0], density_floor)
    ux = u[1] / rs
    uy = u[2] / rs
    temp = jnp.maximum((u[3] - 0.5 * (u[1] * ux + u[2] * uy)) / rs, thermal_lower_bound)
    return rs, ux, uy, temp


def chunk_of(first, c):
    k = first + c * HALF
    i = k // NVY
    j = k % NVY
    vx = -vel_max + (i.astype(f32) + 0.5) * DVX
    vy = -vel_max + (j.astype(f32) + 0.5) * DVY
    return vx, vy, j // HALF, j


def coarse(main, halo):
    nx = main.shape[1]
    rows = nx + 2 * TILE
    u = [jnp.concatenate([halo[0, c], main[c], halo[1, c]], axis=0) for c in range(4)]
    ny = u[0].shape[1]
    rs, ux, uy, temp = physical_variables(u)
    p = rs * temp
    wave = jnp.sqrt(2.0 * temp)
    fx = [u[1], u[1] * ux + p, u[2] * ux, (u[3] + p) * ux]
    fy = [u[2], u[1] * uy, u[2] * uy + p, (u[3] + p) * uy]
    sx = jnp.abs(ux) + wave
    sy = jnp.abs(uy) + wave
    mx = jnp.maximum(sx, pltpu.roll(sx, rows - 1, 0))
    my = jnp.maximum(sy, pltpu.roll(sy, ny - 1, 1))
    out = []
    for c in range(4):
        face_x = 0.5 * (fx[c] + pltpu.roll(fx[c], rows - 1, 0)) - 0.5 * mx * (
            pltpu.roll(u[c], rows - 1, 0) - u[c]
        )
        face_y = 0.5 * (fy[c] + pltpu.roll(fy[c], ny - 1, 1)) - 0.5 * my * (
            pltpu.roll(u[c], ny - 1, 1) - u[c]
        )
        g = u[c] - coarse_ratio * (
            face_x - pltpu.roll(face_x, 1, 0) + (face_y - pltpu.roll(face_y, 1, 1))
        )
        out.append(g[TILE : TILE + nx])
    return out


def advance_kernel(
    nw, nv, owners,
    f, r, star2, corr_out, e_out,
    fpad, spad, s2, rpad, part, red_in, full, uh, vfull, vh, corr, yt, flux, phys, delta,
    load_sem, halo_send, halo_recv, rs_send, rs_recv, ag_send, ag_recv, edge_send, edge_recv,
    win_send, win_recv, out_sem,
):
    w, v, s = lax.axis_index("win"), lax.axis_index("vel"), lax.axis_index("sp")
    count, nx, ny = f.shape
    chunks = count // HALF
    first = v * count
    other = 1 - s
    pos = (2 * v) // nv
    main = pl.ds(2 * TILE, nx)
    end = 2 * TILE + nx
    up = pl.ds(2 * TILE + 1 - 2 * pos, nx)
    hb = pl.multiple_of(end - (end - TILE) * pos, TILE)
    edge = pl.ds(hb, TILE)
    edge_up = pl.ds(hb + 1 - 2 * pos, TILE)
    band = 4 * nx // owners

    def peer(d):
        return lax.rem(v + d, nv)

    load_f = pltpu.make_async_copy(f, fpad.at[:, main], load_sem.at[0])
    load_r = pltpu.make_async_copy(r, rpad.at[main], load_sem.at[1])
    load_f.start()
    load_r.start()

    barrier = pltpu.get_barrier_semaphore()
    for d in range(1, nv):
        pl.semaphore_signal(barrier, inc=1, device_id=(w, peer(d), s), device_id_type=MESH)
    for d in range(nv):
        pl.semaphore_signal(barrier, inc=1, device_id=(w, peer(d), other), device_id_type=MESH)

    @pl.when(w + 1 < nw)
    def _():
        pl.semaphore_signal(barrier, inc=1, device_id=(w + 1, v, s), device_id_type=MESH)
        pl.semaphore_signal(barrier, inc=1, device_id=(w + 1, v, other), device_id_type=MESH)

    @pl.when(w > 0)
    def _():
        pl.semaphore_signal(barrier, inc=1, device_id=(w - 1, v, s), device_id_type=MESH)
        pl.semaphore_signal(barrier, inc=1, device_id=(w - 1, v, other), device_id_type=MESH)

    ends = jnp.where(w > 0, 2, 0) + jnp.where(w + 1 < nw, 2, 0)
    pl.semaphore_wait(barrier, 2 * nv - 1 + ends)

    def remote(src, dst, send, recv, device):
        return pltpu.make_async_remote_copy(
            src_ref=src, dst_ref=dst, send_sem=send, recv_sem=recv,
            device_id=device, device_id_type=MESH,
        )

    source = pl.ds(pl.multiple_of((nx - TILE) * pos, TILE), TILE)
    halos = [
        remote(f.at[:, source], fpad.at[:, edge], halo_send.at[0], halo_recv.at[0], (w, v, other)),
        remote(r.at[pl.ds(0, TILE)], rpad.at[pl.ds(end, TILE)], halo_send.at[1], halo_recv.at[1], (w, v, other)),
        remote(r.at[pl.ds(nx - TILE, TILE)], rpad.at[pl.ds(TILE, TILE)], halo_send.at[2], halo_recv.at[2], (w, v, other)),
    ]
    for copy in halos:
        copy.start()
    part[...] = jnp.zeros_like(part)
    load_f.wait()
    load_r.wait()
    for copy in halos:
        copy.wait()

    def add_moments(ph, vx, a0, a1, a2):
        part[ph, 0] += WEIGHT * a0
        part[ph, 1] += (WEIGHT * vx) * a0
        part[ph, 2] += WEIGHT * a1
        part[ph, 3] += (0.5 * WEIGHT) * (vx * vx * a0 + a2)

    @pl.loop(0, chunks)
    def _(c):
        vx, vy0, half, _j = chunk_of(first, c)
        shift = ny - 1 - (ny - 2) * half
        ca = fine_ratio * jnp.abs(vx)
        zero = jnp.zeros((nx, ny), f32)
        acc = [zero] * 6
        for jj in range(HALF):
            k = c * HALF + jj
            vy = vy0 + jj * DVY
            cb = fine_ratio * jnp.abs(vy)
            cc = 1.0 - ca - cb
            g = fpad[k, main]
            star = cc * g + ca * fpad[k, up] + cb * pltpu.roll(g, shift, 1)
            spad[k, main] = star
            h = fpad[k, edge]
            spad[k, edge] = cc * h + ca * fpad[k, edge_up] + cb * pltpu.roll(h, shift, 1)
            yg, ys = vy * g, vy * star
            acc = [acc[0] + star, acc[1] + ys, acc[2] + vy * ys, acc[3] + g, acc[4] + yg, acc[5] + vy * yg]
        add_moments(0, vx, *acc[:3])
        add_moments(1, vx, *acc[3:])

    def band_of(o):
        row = o * band
        return row // nx, pl.ds(pl.multiple_of(row % nx, TILE), band)

    def scatter(ph):
        for d in range(1, nv):
            def send(d=d):
                comp, rows = band_of(peer(d))
                remote(
                    part.at[ph, comp, rows], red_in.at[ph, d - 1], rs_send.at[ph], rs_recv.at[ph],
                    (w, peer(d), s),
                ).start()

            if owners == nv:
                send()
            else:
                pl.when(peer(d) < owners)(send)

    def owner(fn):
        if owners == nv:
            fn()
        else:
            pl.when(v < owners)(fn)

    def settle(ref, sem):
        pltpu.make_async_copy(ref, ref, sem).wait()

    def gather(ph):
        def go():
            settle(red_in.at[ph], rs_recv.at[ph])
            comp, rows = band_of(v)
            total = part[ph, comp, rows]
            for d in range(1, nv):
                total = total + red_in[ph, d - 1]
            full[ph, comp, rows] = total
            for d in range(1, nv):
                remote(
                    full.at[ph, comp, rows], full.at[ph, comp, rows], ag_send.at[ph], ag_recv.at[ph],
                    (w, peer(d), s),
                ).start()
            if ph < 2:
                row = (v * band) % nx

                @pl.when(row == 0)
                def _():
                    for d in range(nv):
                        remote(
                            full.at[ph, comp, pl.ds(0, TILE)], uh.at[ph, 1, comp],
                            edge_send.at[2 * ph], edge_recv.at[ph], (w, peer(d), other),
                        ).start()

                @pl.when(row + band == nx)
                def _():
                    for d in range(nv):
                        remote(
                            full.at[ph, comp, pl.ds(nx - TILE, TILE)], uh.at[ph, 0, comp],
                            edge_send.at[2 * ph + 1], edge_recv.at[ph], (w, peer(d), other),
                        ).start()

        owner(go)

    def gathered(ph):
        def mine():
            for _ in range(owners - 1):
                settle(red_in.at[ph, 0], ag_recv.at[ph])

        def all_of_them():
            for _ in range(owners):
                settle(red_in.at[ph, 0], ag_recv.at[ph])

        if owners == nv:
            settle(red_in.at[ph], ag_recv.at[ph])
        else:
            pl.when(v < owners)(mine)
            pl.when(v >= owners)(all_of_them)
        if ph < 2:
            settle(uh.at[ph], edge_recv.at[ph])

    scatter(0)
    scatter(1)

    rate = rpad[...]
    inv_main = 1.0 / (1.0 + rpad[main])
    inv_up = 1.0 / (1.0 + rpad[up])
    inv_edge = 1.0 / (1.0 + rpad[edge])

    @pl.loop(0, chunks)
    def _(c):
        vx, vy0, half, _j = chunk_of(first, c)
        shift = ny - 1 - (ny - 2) * half
        ca = fine_ratio * jnp.abs(vx)
        zero = jnp.zeros((nx, ny), f32)
        acc = [zero] * 3
        for jj in range(HALF):
            k = c * HALF + jj
            vy = vy0 + jj * DVY
            cb = fine_ratio * jnp.abs(vy)
            cc = 1.0 - ca - cb
            g = spad[k, main] * inv_main
            star = cc * g + (ca * spad[k, up]) * inv_up + cb * pltpu.roll(g, shift, 1)
            ys = vy * star
            acc = [acc[0] + star, acc[1] + ys, acc[2] + vy * ys]
        add_moments(2, vx, *acc)

    scatter(2)
    gather(0)
    gather(1)
    gather(2)

    gathered(0)
    wide = pl.ds(TILE, nx + 2 * TILE)
    u = [jnp.concatenate([uh[0, 0, c], full[0, c], uh[0, 1, c]], axis=0) for c in range(4)]
    rs, ux, uy, temp = physical_variables(u)
    rate = rpad[wide]
    phys[0, wide] = ux
    phys[1, wide] = uy
    phys[2, wide] = -0.5 / temp
    phys[3, wide] = rs / temp * (rate / (1.0 + rate))

    @pl.loop(1, 3 + nx // TILE)
    def _(t):
        rows = pl.ds(pl.multiple_of(t * TILE, TILE), TILE)
        ux, uy, scale, amp = [phys[n, rows] for n in range(4)]
        zero = jnp.zeros_like(ux)

        def half_sums(speeds, drift, keep):
            sums = {0: [zero] * 4, 1: [zero] * 4}
            for n, speed in enumerate(speeds):
                d = speed - drift
                e = jnp.exp(d * d * scale)
                if keep:
                    yt[n, rows] = e
                side = sums[int(speed > 0)]
                e1 = speed * e
                e2 = speed * e1
                sums[int(speed > 0)] = [side[0] + e, side[1] + e1, side[2] + e2, side[3] + speed * e2]
            return sums[1], sums[0]

        xp, xm = half_sums([-vel_max + (i + 0.5) * DVX for i in range(NVX)], ux, False)
        yp, ym = half_sums([-vel_max + (j + 0.5) * DVY for j in range(NVY)], uy, True)
        xs = [a + b for a, b in zip(xp, xm)]
        ys = [a + b for a, b in zip(yp, ym)]
        amp = WEIGHT * amp

        def store(n, coef, x, y):
            x = [coef * amp * t for t in x]
            flux[n, rows] = x[0] * y[0]
            flux[n + 1, rows] = x[1] * y[0]
            flux[n + 2, rows] = x[0] * y[1]
            flux[n + 3, rows] = 0.5 * (x[2] * y[0] + x[0] * y[2])

        store(0, 1.0, xs, ys)
        store(4, fine_ratio, xp[1:], ys)
        store(8, -fine_ratio, xm[1:], ys)
        store(12, fine_ratio, xs, yp[1:])
        store(16, -fine_ratio, xs, ym[1:])

    gathered(2)
    below, above = pl.ds(2 * TILE - 1, nx), pl.ds(2 * TILE + 1, nx)
    for c in range(4):
        to_y, from_y = flux[12 + c, main], flux[16 + c, main]
        e_out[c] = full[2, c] + (
            flux[c, main] - flux[4 + c, main] - flux[8 + c, main] - to_y - from_y
            + flux[4 + c, below] + flux[8 + c, above]
            + pltpu.roll(to_y, 1, 1) + pltpu.roll(from_y, ny - 1, 1)
        )
    gathered(1)
    stepped = coarse(full.at[1], uh.at[1])
    for c in range(4):
        delta[c] = e_out[c] - stepped[c]

    def onward(n):
        return [
            remote(corr, vfull, win_send.at[0], win_recv.at[0], (n, v, s)),
            remote(corr.at[:, pl.ds(0, TILE)], vh.at[1], win_send.at[1], win_recv.at[1], (n, v, other)),
            remote(corr.at[:, pl.ds(nx - TILE, TILE)], vh.at[0], win_send.at[2], win_recv.at[2], (n, v, other)),
        ]

    def pass_on():
        @pl.when(w + 1 < nw)
        def _():
            for copy in onward(w + 1):
                copy.start()

    @pl.when(w == 0)
    def _():
        for c in range(4):
            corr[c] = stepped[c] + delta[c]
        pass_on()

    @pl.loop(0, chunks)
    def _(c):
        vx, vy0, half, j0 = chunk_of(first, c)
        shift = ny - 1 - (ny - 2) * half
        ca = fine_ratio * jnp.abs(vx)
        dm = vx - phys[0, main]
        xm = phys[3, main] * jnp.exp(dm * dm * phys[2, main])
        de = vx - phys[0, edge]
        xe = phys[3, edge] * jnp.exp(de * de * phys[2, edge])
        for jj in range(HALF):
            k = c * HALF + jj
            fpad[k, main] = spad[k, main] * inv_main + xm * yt[j0 + jj, main]
            fpad[k, edge] = spad[k, edge] * inv_edge + xe * yt[j0 + jj, edge]
        for jj in range(HALF):
            k = c * HALF + jj
            cb = fine_ratio * jnp.abs(vy0 + jj * DVY)
            g = fpad[k, main]
            s2[k] = (1.0 - ca - cb) * g + ca * fpad[k, up] + cb * pltpu.roll(g, shift, 1)

    save = pltpu.make_async_copy(s2, star2, out_sem)
    save.start()

    @pl.when(w > 0)
    def _():
        for copy in onward(w):
            copy.wait_recv()
        moved = coarse(vfull, vh)
        for c in range(4):
            corr[c] = moved[c] + delta[c]
        pass_on()

    corr_out[...] = corr[...]
    save.wait()

    @pl.when(w + 1 < nw)
    def _():
        for copy in onward(w + 1):
            copy.wait_send()

    for ph in range(3):
        if owners == nv:
            settle(red_in.at[ph], rs_send.at[ph])
            settle(red_in.at[ph], ag_send.at[ph])
        else:
            for d in range(1, nv):
                @pl.when(peer(d) < owners)
                def _():
                    settle(red_in.at[ph, 0], rs_send.at[ph])

            def sent():
                settle(red_in.at[ph], ag_send.at[ph])

            pl.when(v < owners)(sent)

    def edges():
        row = (v * band) % nx
        for ph in range(2):
            for side, at_edge in ((0, row == 0), (1, row + band == nx)):
                @pl.when(at_edge)
                def _():
                    for _ in range(nv):
                        settle(uh.at[ph, 0, 0], edge_send.at[2 * ph + side])

    owner(edges)


def lift_kernel(star2, corr, ending, r, lifted, corrected, ye, yc, ph):
    count = star2.shape[0]
    step = pl.program_id(0)
    first = lax.axis_index("vel") * (count * pl.num_programs(0)) + step * count

    @pl.when(step == 0)
    def _():
        corrected[...] = corr[...]
        inv = 1.0 / (1.0 + r[...])
        ph[8] = inv
        for n, (u, table) in enumerate(((ending, ye), (corr, yc))):
            rs, ux, uy, temp = physical_variables(u)
            scale = -0.5 / temp
            amp = rs / temp
            ph[4 * n] = ux
            ph[4 * n + 1] = scale
            ph[4 * n + 2] = amp * inv if n == 0 else amp
            for j in range(NVY):
                d = (-vel_max + (j + 0.5) * DVY) - uy
                table[j] = jnp.exp(d * d * scale)

    inv = ph[8]
    for c in range(count // HALF):
        vx, _vy, _half, j0 = chunk_of(first, c)
        de, dc = vx - ph[0], vx - ph[4]
        xe = ph[2] * jnp.exp(de * de * ph[1])
        xc = ph[6] * jnp.exp(dc * dc * ph[5])
        for jj in range(HALF):
            k = c * HALF + jj
            lifted[k] = star2[k] * inv - xe * ye[j0 + jj] + xc * yc[j0 + jj]


def per_device(nw, nv, f_start, relax_rate):
    field = f_start[0]
    count, nx, ny = field.shape
    owners = min(nv, 4 * nx // TILE)
    band = 4 * nx // owners
    pad = nx + 4 * TILE
    vmem = pltpu.VMEM
    dma = pltpu.SemaphoreType.DMA
    small = jax.ShapeDtypeStruct((4, nx, ny), f32)
    in_vmem = pl.BlockSpec(memory_space=pltpu.VMEM)
    anywhere = pl.BlockSpec(memory_space=pl.ANY)
    star2, corr, ending = pl.pallas_call(
        functools.partial(advance_kernel, nw, nv, owners),
        out_shape=(jax.ShapeDtypeStruct((count, nx, ny), f32), small, small),
        in_specs=[anywhere, anywhere],
        out_specs=(anywhere, in_vmem, in_vmem),
        scratch_shapes=[
            vmem((count, pad, ny), f32),
            vmem((count, pad, ny), f32),
            vmem((count, nx, ny), f32),
            vmem((pad, ny), f32),
            vmem((3, 4, nx, ny), f32),
            vmem((3, nv - 1, band, ny), f32),
            vmem((3, 4, nx, ny), f32),
            vmem((2, 2, 4, TILE, ny), f32),
            vmem((4, nx, ny), f32),
            vmem((2, 4, TILE, ny), f32),
            vmem((4, nx, ny), f32),
            vmem((NVY, pad, ny), f32),
            vmem((20, pad, ny), f32),
            vmem((4, pad, ny), f32),
            vmem((4, nx, ny), f32),
            dma((2,)), dma((3,)), dma((3,)), dma((3,)), dma((3,)), dma((3,)), dma((3,)),
            dma((4,)), dma((2,)), dma((3,)), dma((3,)), dma,
        ],
        compiler_params=pltpu.CompilerParams(
            collective_id=0, has_side_effects=True, vmem_limit_bytes=40 << 20
        ),
        name="advance",
    )(field, relax_rate)

    block = 2 * HALF if count % (2 * HALF) == 0 else HALF
    whole = pl.BlockSpec((4, nx, ny), lambda i: (0, 0, 0))
    slab = pl.BlockSpec((block, nx, ny), lambda i: (i, 0, 0))
    lifted, corrected = pl.pallas_call(
        lift_kernel,
        grid=(count // block,),
        out_shape=(jax.ShapeDtypeStruct((count, nx, ny), f32), small),
        in_specs=[slab, whole, whole, pl.BlockSpec((nx, ny), lambda i: (0, 0))],
        out_specs=(slab, whole),
        scratch_shapes=[vmem((NVY, nx, ny), f32), vmem((NVY, nx, ny), f32), vmem((9, nx, ny), f32)],
        name="lift",
    )(star2, corr, ending, relax_rate)
    return corrected[None], lifted[None]


def solution(mesh):
    return jax.shard_map(
        functools.partial(per_device, mesh.shape["win"], mesh.shape["vel"]),
        mesh=mesh,
        in_specs=(P("win", "vel", "sp", None), P("sp", None)),
        out_specs=(P("win", None, "sp", None), P("win", "vel", "sp", None)),
        check_vma=False,
    )
```

```python
import functools
import math

import jax
import jax.numpy as jnp
from jax import lax
from jax.experimental import pallas as pl
from jax.experimental.pallas import tpu as pltpu
from jax.sharding import PartitionSpec as P

NVX = 48
NVY = 32
HALF = NVY // 2
TILE = 8
vel_max = 6.0
fine_ratio = 0.075
coarse_ratio = 0.15
density_floor = 0.3
thermal_lower_bound = 0.3
DVX = 2.0 * vel_max / NVX
DVY = 2.0 * vel_max / NVY
WEIGHT = DVX * DVY / (2.0 * math.pi)
MESH = pl.DeviceIdType.MESH
f32 = jnp.float32


def physical_variables(u):
    rs = jnp.maximum(u[0], density_floor)
    ux = u[1] / rs
    uy = u[2] / rs
    temp = jnp.maximum((u[3] - 0.5 * (u[1] * ux + u[2] * uy)) / rs, thermal_lower_bound)
    return rs, ux, uy, temp


def chunk_of(first, c):
    k = first + c * HALF
    i = k // NVY
    j = k % NVY
    vx = -vel_max + (i.astype(f32) + 0.5) * DVX
    vy = -vel_max + (j.astype(f32) + 0.5) * DVY
    return vx, vy, j // HALF, j


def coarse(main, halo):
    nx = main.shape[1]
    rows = nx + 2 * TILE
    u = [jnp.concatenate([halo[0, c], main[c], halo[1, c]], axis=0) for c in range(4)]
    ny = u[0].shape[1]
    rs, ux, uy, temp = physical_variables(u)
    p = rs * temp
    wave = jnp.sqrt(2.0 * temp)
    fx = [u[1], u[1] * ux + p, u[2] * ux, (u[3] + p) * ux]
    fy = [u[2], u[1] * uy, u[2] * uy + p, (u[3] + p) * uy]
    sx = jnp.abs(ux) + wave
    sy = jnp.abs(uy) + wave
    mx = jnp.maximum(sx, pltpu.roll(sx, rows - 1, 0))
    my = jnp.maximum(sy, pltpu.roll(sy, ny - 1, 1))
    out = []
    for c in range(4):
        face_x = 0.5 * (fx[c] + pltpu.roll(fx[c], rows - 1, 0)) - 0.5 * mx * (
            pltpu.roll(u[c], rows - 1, 0) - u[c]
        )
        face_y = 0.5 * (fy[c] + pltpu.roll(fy[c], ny - 1, 1)) - 0.5 * my * (
            pltpu.roll(u[c], ny - 1, 1) - u[c]
        )
        g = u[c] - coarse_ratio * (
            face_x - pltpu.roll(face_x, 1, 0) + (face_y - pltpu.roll(face_y, 1, 1))
        )
        out.append(g[TILE : TILE + nx])
    return out


def advance_kernel(
    nw, nv, owners,
    f, r, star2, corr_out, e_out,
    fpad, spad, rpad, part, red_in, full, uh, vfull, vh, corr, yt, flux, phys, delta,
    load_sem, halo_send, halo_recv, rs_send, rs_recv, ag_send, ag_recv, edge_send, edge_recv,
    win_send, win_recv,
):
    w, v, s = lax.axis_index("win"), lax.axis_index("vel"), lax.axis_index("sp")
    count, nx, ny = f.shape
    chunks = count // HALF
    first = v * count
    other = 1 - s
    pos = (2 * v) // nv
    main = pl.ds(2 * TILE, nx)
    end = 2 * TILE + nx
    up = pl.ds(2 * TILE + 1 - 2 * pos, nx)
    hb = pl.multiple_of(end - (end - TILE) * pos, TILE)
    edge = pl.ds(hb, TILE)
    edge_up = pl.ds(hb + 1 - 2 * pos, TILE)
    band = 4 * nx // owners

    def peer(d):
        return lax.rem(v + d, nv)

    load_f = pltpu.make_async_copy(f, fpad.at[:, main], load_sem.at[0])
    load_r = pltpu.make_async_copy(r, rpad.at[main], load_sem.at[1])
    load_f.start()
    load_r.start()

    barrier = pltpu.get_barrier_semaphore()
    for d in range(1, nv):
        pl.semaphore_signal(barrier, inc=1, device_id=(w, peer(d), s), device_id_type=MESH)
    for d in range(nv):
        pl.semaphore_signal(barrier, inc=1, device_id=(w, peer(d), other), device_id_type=MESH)

    @pl.when(w + 1 < nw)
    def _():
        pl.semaphore_signal(barrier, inc=1, device_id=(w + 1, v, s), device_id_type=MESH)
        pl.semaphore_signal(barrier, inc=1, device_id=(w + 1, v, other), device_id_type=MESH)

    @pl.when(w > 0)
    def _():
        pl.semaphore_signal(barrier, inc=1, device_id=(w - 1, v, s), device_id_type=MESH)
        pl.semaphore_signal(barrier, inc=1, device_id=(w - 1, v, other), device_id_type=MESH)

    ends = jnp.where(w > 0, 2, 0) + jnp.where(w + 1 < nw, 2, 0)
    pl.semaphore_wait(barrier, 2 * nv - 1 + ends)

    def remote(src, dst, send, recv, device):
        return pltpu.make_async_remote_copy(
            src_ref=src, dst_ref=dst, send_sem=send, recv_sem=recv,
            device_id=device, device_id_type=MESH,
        )

    source = pl.ds(pl.multiple_of((nx - TILE) * pos, TILE), TILE)
    halos = [
        remote(f.at[:, source], fpad.at[:, edge], halo_send.at[0], halo_recv.at[0], (w, v, other)),
        remote(r.at[pl.ds(0, TILE)], rpad.at[pl.ds(end, TILE)], halo_send.at[1], halo_recv.at[1], (w, v, other)),
        remote(r.at[pl.ds(nx - TILE, TILE)], rpad.at[pl.ds(TILE, TILE)], halo_send.at[2], halo_recv.at[2], (w, v, other)),
    ]
    for copy in halos:
        copy.start()
    part[...] = jnp.zeros_like(part)
    load_f.wait()
    load_r.wait()
    for copy in halos:
        copy.wait()

    def add_moments(ph, vx, a0, a1, a2):
        part[ph, 0] += WEIGHT * a0
        part[ph, 1] += (WEIGHT * vx) * a0
        part[ph, 2] += WEIGHT * a1
        part[ph, 3] += (0.5 * WEIGHT) * (vx * vx * a0 + a2)

    @pl.loop(0, chunks)
    def _(c):
        vx, vy0, half, _j = chunk_of(first, c)
        shift = ny - 1 - (ny - 2) * half
        ca = fine_ratio * jnp.abs(vx)
        zero = jnp.zeros((nx, ny), f32)
        acc = [zero] * 6
        for jj in range(HALF):
            k = c * HALF + jj
            vy = vy0 + jj * DVY
            cb = fine_ratio * jnp.abs(vy)
            cc = 1.0 - ca - cb
            g = fpad[k, main]
            star = cc * g + ca * fpad[k, up] + cb * pltpu.roll(g, shift, 1)
            spad[k, main] = star
            h = fpad[k, edge]
            spad[k, edge] = cc * h + ca * fpad[k, edge_up] + cb * pltpu.roll(h, shift, 1)
            yg, ys = vy * g, vy * star
            acc = [acc[0] + star, acc[1] + ys, acc[2] + vy * ys, acc[3] + g, acc[4] + yg, acc[5] + vy * yg]
        add_moments(0, vx, *acc[:3])
        add_moments(1, vx, *acc[3:])

    def band_of(o):
        row = o * band
        return row // nx, pl.ds(pl.multiple_of(row % nx, TILE), band)

    def scatter(ph):
        for d in range(1, nv):
            def send(d=d):
                comp, rows = band_of(peer(d))
                remote(
                    part.at[ph, comp, rows], red_in.at[ph, d - 1], rs_send.at[ph], rs_recv.at[ph],
                    (w, peer(d), s),
                ).start()

            if owners == nv:
                send()
            else:
                pl.when(peer(d) < owners)(send)

    def owner(fn):
        if owners == nv:
            fn()
        else:
            pl.when(v < owners)(fn)

    def settle(ref, sem):
        pltpu.make_async_copy(ref, ref, sem).wait()

    def gather(ph):
        def go():
            settle(red_in.at[ph], rs_recv.at[ph])
            comp, rows = band_of(v)
            total = part[ph, comp, rows]
            for d in range(1, nv):
                total = total + red_in[ph, d - 1]
            full[ph, comp, rows] = total
            for d in range(1, nv):
                remote(
                    full.at[ph, comp, rows], full.at[ph, comp, rows], ag_send.at[ph], ag_recv.at[ph],
                    (w, peer(d), s),
                ).start()
            if ph < 2:
                row = (v * band) % nx

                @pl.when(row == 0)
                def _():
                    for d in range(nv):
                        remote(
                            full.at[ph, comp, pl.ds(0, TILE)], uh.at[ph, 1, comp],
                            edge_send.at[2 * ph], edge_recv.at[ph], (w, peer(d), other),
                        ).start()

                @pl.when(row + band == nx)
                def _():
                    for d in range(nv):
                        remote(
                            full.at[ph, comp, pl.ds(nx - TILE, TILE)], uh.at[ph, 0, comp],
                            edge_send.at[2 * ph + 1], edge_recv.at[ph], (w, peer(d), other),
                        ).start()

        owner(go)

    def gathered(ph):
        def mine():
            for _ in range(owners - 1):
                settle(red_in.at[ph, 0], ag_recv.at[ph])

        def all_of_them():
            for _ in range(owners):
                settle(red_in.at[ph, 0], ag_recv.at[ph])

        if owners == nv:
            settle(red_in.at[ph], ag_recv.at[ph])
        else:
            pl.when(v < owners)(mine)
            pl.when(v >= owners)(all_of_them)
        if ph < 2:
            settle(uh.at[ph], edge_recv.at[ph])

    scatter(0)
    scatter(1)

    rate = rpad[...]
    inv_main = 1.0 / (1.0 + rpad[main])
    inv_up = 1.0 / (1.0 + rpad[up])
    inv_edge = 1.0 / (1.0 + rpad[edge])

    @pl.loop(0, chunks)
    def _(c):
        vx, vy0, half, _j = chunk_of(first, c)
        shift = ny - 1 - (ny - 2) * half
        ca = fine_ratio * jnp.abs(vx)
        zero = jnp.zeros((nx, ny), f32)
        acc = [zero] * 3
        for jj in range(HALF):
            k = c * HALF + jj
            vy = vy0 + jj * DVY
            cb = fine_ratio * jnp.abs(vy)
            cc = 1.0 - ca - cb
            g = spad[k, main] * inv_main
            star = cc * g + (ca * spad[k, up]) * inv_up + cb * pltpu.roll(g, shift, 1)
            ys = vy * star
            acc = [acc[0] + star, acc[1] + ys, acc[2] + vy * ys]
        add_moments(2, vx, *acc)

    scatter(2)
    gather(0)
    gather(1)
    gather(2)

    gathered(0)
    wide = pl.ds(TILE, nx + 2 * TILE)
    u = [jnp.concatenate([uh[0, 0, c], full[0, c], uh[0, 1, c]], axis=0) for c in range(4)]
    rs, ux, uy, temp = physical_variables(u)
    rate = rpad[wide]
    phys[0, wide] = ux
    phys[1, wide] = uy
    phys[2, wide] = -0.5 / temp
    phys[3, wide] = rs / temp * (rate / (1.0 + rate))

    @pl.loop(1, 3 + nx // TILE)
    def _(t):
        rows = pl.ds(pl.multiple_of(t * TILE, TILE), TILE)
        ux, uy, scale, amp = [phys[n, rows] for n in range(4)]
        zero = jnp.zeros_like(ux)

        def half_sums(speeds, drift, keep):
            sums = {0: [zero] * 4, 1: [zero] * 4}
            for n, speed in enumerate(speeds):
                d = speed - drift
                e = jnp.exp(d * d * scale)
                if keep:
                    yt[n, rows] = e
                side = sums[int(speed > 0)]
                e1 = speed * e
                e2 = speed * e1
                sums[int(speed > 0)] = [side[0] + e, side[1] + e1, side[2] + e2, side[3] + speed * e2]
            return sums[1], sums[0]

        xp, xm = half_sums([-vel_max + (i + 0.5) * DVX for i in range(NVX)], ux, False)
        yp, ym = half_sums([-vel_max + (j + 0.5) * DVY for j in range(NVY)], uy, True)
        xs = [a + b for a, b in zip(xp, xm)]
        ys = [a + b for a, b in zip(yp, ym)]
        amp = WEIGHT * amp

        def store(n, coef, x, y):
            x = [coef * amp * t for t in x]
            flux[n, rows] = x[0] * y[0]
            flux[n + 1, rows] = x[1] * y[0]
            flux[n + 2, rows] = x[0] * y[1]
            flux[n + 3, rows] = 0.5 * (x[2] * y[0] + x[0] * y[2])

        store(0, 1.0, xs, ys)
        store(4, fine_ratio, xp[1:], ys)
        store(8, -fine_ratio, xm[1:], ys)
        store(12, fine_ratio, xs, yp[1:])
        store(16, -fine_ratio, xs, ym[1:])

    gathered(2)
    below, above = pl.ds(2 * TILE - 1, nx), pl.ds(2 * TILE + 1, nx)
    for c in range(4):
        to_y, from_y = flux[12 + c, main], flux[16 + c, main]
        e_out[c] = full[2, c] + (
            flux[c, main] - flux[4 + c, main] - flux[8 + c, main] - to_y - from_y
            + flux[4 + c, below] + flux[8 + c, above]
            + pltpu.roll(to_y, 1, 1) + pltpu.roll(from_y, ny - 1, 1)
        )
    gathered(1)
    stepped = coarse(full.at[1], uh.at[1])
    for c in range(4):
        delta[c] = e_out[c] - stepped[c]

    def onward(n):
        return [
            remote(corr, vfull, win_send.at[0], win_recv.at[0], (n, v, s)),
            remote(corr.at[:, pl.ds(0, TILE)], vh.at[1], win_send.at[1], win_recv.at[1], (n, v, other)),
            remote(corr.at[:, pl.ds(nx - TILE, TILE)], vh.at[0], win_send.at[2], win_recv.at[2], (n, v, other)),
        ]

    def pass_on():
        @pl.when(w + 1 < nw)
        def _():
            for copy in onward(w + 1):
                copy.start()

    @pl.when(w == 0)
    def _():
        for c in range(4):
            corr[c] = stepped[c] + delta[c]
        pass_on()

    @pl.loop(0, chunks)
    def _(c):
        vx, vy0, half, j0 = chunk_of(first, c)
        shift = ny - 1 - (ny - 2) * half
        ca = fine_ratio * jnp.abs(vx)
        dm = vx - phys[0, main]
        xm = phys[3, main] * jnp.exp(dm * dm * phys[2, main])
        de = vx - phys[0, edge]
        xe = phys[3, edge] * jnp.exp(de * de * phys[2, edge])
        for jj in range(HALF):
            k = c * HALF + jj
            fpad[k, main] = spad[k, main] * inv_main + xm * yt[j0 + jj, main]
            fpad[k, edge] = spad[k, edge] * inv_edge + xe * yt[j0 + jj, edge]
        for jj in range(HALF):
            k = c * HALF + jj
            cb = fine_ratio * jnp.abs(vy0 + jj * DVY)
            g = fpad[k, main]
            star2[k] = (1.0 - ca - cb) * g + ca * fpad[k, up] + cb * pltpu.roll(g, shift, 1)

    @pl.when(w > 0)
    def _():
        for copy in onward(w):
            copy.wait_recv()
        moved = coarse(vfull, vh)
        for c in range(4):
            corr[c] = moved[c] + delta[c]
        pass_on()

    corr_out[...] = corr[...]

    @pl.when(w + 1 < nw)
    def _():
        for copy in onward(w + 1):
            copy.wait_send()

    for ph in range(3):
        if owners == nv:
            settle(red_in.at[ph], rs_send.at[ph])
            settle(red_in.at[ph], ag_send.at[ph])
        else:
            for d in range(1, nv):
                @pl.when(peer(d) < owners)
                def _():
                    settle(red_in.at[ph, 0], rs_send.at[ph])

            def sent():
                settle(red_in.at[ph], ag_send.at[ph])

            pl.when(v < owners)(sent)

    def edges():
        row = (v * band) % nx
        for ph in range(2):
            for side, at_edge in ((0, row == 0), (1, row + band == nx)):
                @pl.when(at_edge)
                def _():
                    for _ in range(nv):
                        settle(uh.at[ph, 0, 0], edge_send.at[2 * ph + side])

    owner(edges)


def lift_kernel(parts, star2, corr, ending, r, lifted, corrected, ye, yc, out, save_sem):
    count = star2.shape[0]
    first = lax.axis_index("vel") * count
    corrected[...] = corr[...]
    inv = 1.0 / (1.0 + r[...])
    sides = []
    for u, table in ((ending, ye), (corr, yc)):
        rs, ux, uy, temp = physical_variables(u)
        scale = -0.5 / temp
        amp = rs / temp
        sides.append((ux, scale, amp))
        for j in range(NVY):
            d = (-vel_max + (j + 0.5) * DVY) - uy
            table[j] = jnp.exp(d * d * scale)
    (ue, se, me), (uc, sc, mc) = sides
    me = me * inv
    chunks = count // HALF
    per = chunks // parts

    def save(n):
        rows = pl.ds(n * per * HALF, per * HALF)
        return pltpu.make_async_copy(out.at[rows], lifted.at[rows], save_sem.at[n])

    for n in range(parts):

        @pl.loop(n * per, (n + 1) * per)
        def _(c):
            vx, _vy, _half, j0 = chunk_of(first, c)
            de, dc = vx - ue, vx - uc
            xe = me * jnp.exp(de * de * se)
            xc = mc * jnp.exp(dc * dc * sc)
            for jj in range(HALF):
                k = c * HALF + jj
                out[k] = star2[k] * inv - xe * ye[j0 + jj] + xc * yc[j0 + jj]

        save(n).start()
    for n in range(parts):
        save(n).wait()


def per_device(nw, nv, f_start, relax_rate):
    field = f_start[0]
    count, nx, ny = field.shape
    owners = min(nv, 4 * nx // TILE)
    band = 4 * nx // owners
    pad = nx + 4 * TILE
    vmem = pltpu.VMEM
    dma = pltpu.SemaphoreType.DMA
    small = jax.ShapeDtypeStruct((4, nx, ny), f32)
    in_vmem = pl.BlockSpec(memory_space=pltpu.VMEM)
    in_hbm = pl.BlockSpec(memory_space=pltpu.HBM)
    field = pltpu.with_memory_space_constraint(field, pltpu.HBM)
    star2, corr, ending = pl.pallas_call(
        functools.partial(advance_kernel, nw, nv, owners),
        out_shape=(jax.ShapeDtypeStruct((count, nx, ny), f32), small, small),
        in_specs=[in_hbm, in_hbm],
        out_specs=(in_vmem, in_vmem, in_vmem),
        scratch_shapes=[
            vmem((count, pad, ny), f32),
            vmem((count, pad, ny), f32),
            vmem((pad, ny), f32),
            vmem((3, 4, nx, ny), f32),
            vmem((3, nv - 1, band, ny), f32),
            vmem((3, 4, nx, ny), f32),
            vmem((2, 2, 4, TILE, ny), f32),
            vmem((4, nx, ny), f32),
            vmem((2, 4, TILE, ny), f32),
            vmem((4, nx, ny), f32),
            vmem((NVY, pad, ny), f32),
            vmem((20, pad, ny), f32),
            vmem((4, pad, ny), f32),
            vmem((4, nx, ny), f32),
            dma((2,)), dma((3,)), dma((3,)), dma((3,)), dma((3,)), dma((3,)), dma((3,)),
            dma((4,)), dma((2,)), dma((3,)), dma((3,)),
        ],
        compiler_params=pltpu.CompilerParams(
            collective_id=0, has_side_effects=True, vmem_limit_bytes=40 << 20
        ),
        name="advance",
    )(field, pltpu.with_memory_space_constraint(relax_rate, pltpu.HBM))

    chunks = count // HALF
    parts = next(n for n in (6, 4, 3, 2, 1) if chunks % n == 0)
    lifted, corrected = pl.pallas_call(
        functools.partial(lift_kernel, parts),
        out_shape=(jax.ShapeDtypeStruct((count, nx, ny), f32), small),
        in_specs=[in_vmem] * 4,
        out_specs=(in_hbm, in_vmem),
        scratch_shapes=[
            vmem((NVY, nx, ny), f32), vmem((NVY, nx, ny), f32), vmem((count, nx, ny), f32), dma((parts,)),
        ],
        compiler_params=pltpu.CompilerParams(vmem_limit_bytes=16 << 20),
        name="lift",
    )(star2, corr, ending, relax_rate)
    return corrected[None], lifted[None]


def solution(mesh):
    return jax.shard_map(
        functools.partial(per_device, mesh.shape["win"], mesh.shape["vel"]),
        mesh=mesh,
        in_specs=(P("win", "vel", "sp", None), P("sp", None)),
        out_specs=(P("win", None, "sp", None), P("win", "vel", "sp", None)),
        check_vma=False,
    )
```

```python
import functools
import math

import jax
import jax.numpy as jnp
from jax import lax
from jax.experimental import pallas as pl
from jax.experimental.pallas import tpu as pltpu
from jax.sharding import PartitionSpec as P

NVX = 48
NVY = 32
HALF = NVY // 2
TILE = 8
vel_max = 6.0
fine_ratio = 0.075
coarse_ratio = 0.15
density_floor = 0.3
thermal_lower_bound = 0.3
DVX = 2.0 * vel_max / NVX
DVY = 2.0 * vel_max / NVY
WEIGHT = DVX * DVY / (2.0 * math.pi)
MESH = pl.DeviceIdType.MESH
f32 = jnp.float32
ORDERS = [(p, q) for p in range(5) for q in range(5 - p)]
PLACE = {order: n for n, order in enumerate(ORDERS)}


def physical_variables(u):
    rs = jnp.maximum(u[0], density_floor)
    ux = u[1] / rs
    uy = u[2] / rs
    temp = jnp.maximum((u[3] - 0.5 * (u[1] * ux + u[2] * uy)) / rs, thermal_lower_bound)
    return rs, ux, uy, temp


def chunk_of(first, c):
    k = first + c * HALF
    i = k // NVY
    j = k % NVY
    vx = -vel_max + (i.astype(f32) + 0.5) * DVX
    vy = -vel_max + (j.astype(f32) + 0.5) * DVY
    return vx, vy, j // HALF, j


def coarse(main, halo):
    nx = main.shape[1]
    rows = nx + 2 * TILE
    u = [jnp.concatenate([halo[0, c], main[c], halo[1, c]], axis=0) for c in range(4)]
    ny = u[0].shape[1]
    rs, ux, uy, temp = physical_variables(u)
    p = rs * temp
    wave = jnp.sqrt(2.0 * temp)
    fx = [u[1], u[1] * ux + p, u[2] * ux, (u[3] + p) * ux]
    fy = [u[2], u[1] * uy, u[2] * uy + p, (u[3] + p) * uy]
    sx = jnp.abs(ux) + wave
    sy = jnp.abs(uy) + wave
    mx = jnp.maximum(sx, pltpu.roll(sx, rows - 1, 0))
    my = jnp.maximum(sy, pltpu.roll(sy, ny - 1, 1))
    out = []
    for c in range(4):
        face_x = 0.5 * (fx[c] + pltpu.roll(fx[c], rows - 1, 0)) - 0.5 * mx * (
            pltpu.roll(u[c], rows - 1, 0) - u[c]
        )
        face_y = 0.5 * (fy[c] + pltpu.roll(fy[c], ny - 1, 1)) - 0.5 * my * (
            pltpu.roll(u[c], ny - 1, 1) - u[c]
        )
        g = u[c] - coarse_ratio * (
            face_x - pltpu.roll(face_x, 1, 0) + (face_y - pltpu.roll(face_y, 1, 1))
        )
        out.append(g[TILE : TILE + nx])
    return out


def advance_kernel(
    nw, nv, owners,
    f, r, star2, corr_out, e_out,
    fpad, spad, rpad, bsum, hsum, part, red_in, full, uh, vfull, vh, corr, yt, flux, phys, delta,
    load_sem, halo_send, halo_recv, rs_send, rs_recv, ag_send, ag_recv, edge_send, edge_recv,
    win_send, win_recv,
):
    w, v, s = lax.axis_index("win"), lax.axis_index("vel"), lax.axis_index("sp")
    count, nx, ny = f.shape
    chunks = count // HALF
    first = v * count
    other = 1 - s
    pos = (2 * v) // nv
    main = pl.ds(2 * TILE, nx)
    end = 2 * TILE + nx
    up = pl.ds(2 * TILE + 1 - 2 * pos, nx)
    hb = pl.multiple_of(end - (end - TILE) * pos, TILE)
    edge = pl.ds(hb, TILE)
    edge_up = pl.ds(hb + 1 - 2 * pos, TILE)
    band = 4 * nx // owners

    def peer(d):
        return lax.rem(v + d, nv)

    load_f = pltpu.make_async_copy(f, fpad.at[:, main], load_sem.at[0])
    load_r = pltpu.make_async_copy(r, rpad.at[main], load_sem.at[1])
    load_f.start()
    load_r.start()

    barrier = pltpu.get_barrier_semaphore()
    for d in range(1, nv):
        pl.semaphore_signal(barrier, inc=1, device_id=(w, peer(d), s), device_id_type=MESH)
    for d in range(nv):
        pl.semaphore_signal(barrier, inc=1, device_id=(w, peer(d), other), device_id_type=MESH)

    @pl.when(w + 1 < nw)
    def _():
        pl.semaphore_signal(barrier, inc=1, device_id=(w + 1, v, s), device_id_type=MESH)
        pl.semaphore_signal(barrier, inc=1, device_id=(w + 1, v, other), device_id_type=MESH)

    @pl.when(w > 0)
    def _():
        pl.semaphore_signal(barrier, inc=1, device_id=(w - 1, v, s), device_id_type=MESH)
        pl.semaphore_signal(barrier, inc=1, device_id=(w - 1, v, other), device_id_type=MESH)

    def remote(src, dst, send, recv, device):
        return pltpu.make_async_remote_copy(
            src_ref=src, dst_ref=dst, send_sem=send, recv_sem=recv,
            device_id=device, device_id_type=MESH,
        )

    def band_of(o):
        row = o * band
        return row // nx, pl.ds(pl.multiple_of(row % nx, TILE), band)

    def scatter(ph):
        for d in range(1, nv):
            def send(d=d):
                comp, rows = band_of(peer(d))
                remote(
                    part.at[ph, comp, rows], red_in.at[ph, d - 1], rs_send.at[ph], rs_recv.at[ph],
                    (w, peer(d), s),
                ).start()

            if owners == nv:
                send()
            else:
                pl.when(peer(d) < owners)(send)

    def owner(fn):
        if owners == nv:
            fn()
        else:
            pl.when(v < owners)(fn)

    def settle(ref, sem):
        pltpu.make_async_copy(ref, ref, sem).wait()

    def gather(ph):
        def go():
            settle(red_in.at[ph], rs_recv.at[ph])
            comp, rows = band_of(v)
            total = part[ph, comp, rows]
            for d in range(1, nv):
                total = total + red_in[ph, d - 1]
            full[ph, comp, rows] = total
            for d in range(1, nv):
                remote(
                    full.at[ph, comp, rows], full.at[ph, comp, rows], ag_send.at[ph], ag_recv.at[ph],
                    (w, peer(d), s),
                ).start()
            if ph < 2:
                row = (v * band) % nx

                @pl.when(row == 0)
                def _():
                    for d in range(nv):
                        remote(
                            full.at[ph, comp, pl.ds(0, TILE)], uh.at[ph, 1, comp],
                            edge_send.at[2 * ph], edge_recv.at[ph], (w, peer(d), other),
                        ).start()

                @pl.when(row + band == nx)
                def _():
                    for d in range(nv):
                        remote(
                            full.at[ph, comp, pl.ds(nx - TILE, TILE)], uh.at[ph, 0, comp],
                            edge_send.at[2 * ph + 1], edge_recv.at[ph], (w, peer(d), other),
                        ).start()

        owner(go)

    def gathered(ph):
        def mine():
            for _ in range(owners - 1):
                settle(red_in.at[ph, 0], ag_recv.at[ph])

        def all_of_them():
            for _ in range(owners):
                settle(red_in.at[ph, 0], ag_recv.at[ph])

        if owners == nv:
            settle(red_in.at[ph], ag_recv.at[ph])
        else:
            pl.when(v < owners)(mine)
            pl.when(v >= owners)(all_of_them)
        if ph < 2:
            settle(uh.at[ph], edge_recv.at[ph])

    load_f.wait()
    parity = (first // HALF) % 2
    rounds = (chunks + 1) // 2

    @pl.loop(0, nx // TILE)
    def _(t):
        rows = pl.ds(pl.multiple_of(2 * TILE + t * TILE, TILE), TILE)
        for h in range(2):
            acc = {order: jnp.zeros((TILE, ny), f32) for order in ORDERS}
            for n in range(rounds):
                c = (h + parity) % 2 + 2 * n
                weight = 1.0
                if chunks % 2:
                    weight = jnp.where(c < chunks, 1.0, 0.0).astype(f32)
                    c = jnp.minimum(c, chunks - 1)
                vx = chunk_of(first, c)[0]
                sums = [jnp.zeros((TILE, ny), f32)] * 5
                for jj in range(HALF // 2, HALF):
                    tt = (jj + 0.5) * DVY - 0.5 * vel_max
                    high = fpad[c * HALF + jj, rows]
                    low = fpad[c * HALF + HALF - 1 - jj, rows]
                    even, odd = high + low, high - low
                    sums = [
                        sums[0] + even, sums[1] + tt * odd, sums[2] + tt**2 * even,
                        sums[3] + tt**3 * odd, sums[4] + tt**4 * even,
                    ]
                power = weight
                for q in range(5):
                    for m in range(5 - q):
                        term = sums[m] if q == 0 and chunks % 2 == 0 else sums[m] * power
                        acc[m, q] = acc[m, q] + term
                    power = power * vx
            centre = (h - 0.5) * vel_max
            for p, q in ORDERS:
                total = acc[p, q]
                for m in range(p):
                    total = total + (math.comb(p, m) * centre ** (p - m)) * acc[m, q]
                bsum[h, PLACE[p, q], rows] = total

    def components(ph, get):
        part[ph, 0] = WEIGHT * get(0, 0)
        part[ph, 1] = WEIGHT * get(0, 1)
        part[ph, 2] = WEIGHT * get(1, 0)
        part[ph, 3] = (0.5 * WEIGHT) * (get(0, 2) + get(2, 0))

    components(1, lambda p, q: bsum[0, PLACE[p, q], main] + bsum[1, PLACE[p, q], main])

    ends = jnp.where(w > 0, 2, 0) + jnp.where(w + 1 < nw, 2, 0)
    pl.semaphore_wait(barrier, 2 * nv - 1 + ends)
    load_r.wait()

    source = pl.ds(pl.multiple_of((nx - TILE) * pos, TILE), TILE)
    kept = pl.ds(pl.multiple_of(2 * TILE + (nx - TILE) * pos, TILE), TILE)
    halos = [
        remote(bsum.at[:, :, kept], bsum.at[:, :, edge], halo_send.at[3], halo_recv.at[3], (w, v, other)),
        remote(r.at[pl.ds(0, TILE)], rpad.at[pl.ds(end, TILE)], halo_send.at[1], halo_recv.at[1], (w, v, other)),
        remote(r.at[pl.ds(nx - TILE, TILE)], rpad.at[pl.ds(TILE, TILE)], halo_send.at[2], halo_recv.at[2], (w, v, other)),
        remote(f.at[:, source], fpad.at[:, edge], halo_send.at[0], halo_recv.at[0], (w, v, other)),
    ]
    for copy in halos:
        copy.start()
    scatter(1)
    for copy in halos[:3]:
        copy.wait()

    inv_main = 1.0 / (1.0 + rpad[main])
    inv_edge = 1.0 / (1.0 + rpad[edge])
    along = fine_ratio * (2 * pos - 1).astype(f32)
    ACROSS = ((-fine_ratio, ny - 1), (fine_ratio, 1))
    MAIN = [(0, 0), (0, 1), (1, 0), (0, 2), (2, 0)]

    def moved(table, h, p, q, rows, rows_up):
        across, shift = ACROSS[h]
        bx = table[h, PLACE[p, q + 1], rows]
        by = table[h, PLACE[p + 1, q], rows]
        return (
            table[h, PLACE[p, q], rows]
            + along * (table[h, PLACE[p, q + 1], rows_up] - bx)
            + across * (pltpu.roll(by, shift, 1) - by)
        )

    first_star = {}
    for h in range(2):
        for p, q in ORDERS:
            if p + q < 4:
                star = moved(bsum, h, p, q, main, up)
                if (p, q) in MAIN:
                    first_star[p, q] = star + first_star[p, q] if h else star
                hsum[h, PLACE[p, q], main] = star * inv_main
        for p, q in MAIN:
            hsum[h, PLACE[p, q + 1], edge] = moved(bsum, h, p, q + 1, edge, edge_up) * inv_edge
    components(0, lambda p, q: first_star[p, q])
    scatter(0)
    again = {
        order: moved(hsum, 0, *order, main, up) + moved(hsum, 1, *order, main, up) for order in MAIN
    }
    components(2, lambda p, q: again[p, q])
    scatter(2)

    halos[3].wait()

    @pl.loop(0, chunks)
    def _(c):
        vx, vy0, half, _j = chunk_of(first, c)
        shift = ny - 1 - (ny - 2) * half
        ca = fine_ratio * jnp.abs(vx)
        for jj in range(HALF):
            k = c * HALF + jj
            cb = fine_ratio * jnp.abs(vy0 + jj * DVY)
            cc = 1.0 - ca - cb
            g = fpad[k, main]
            spad[k, main] = (cc * g + ca * fpad[k, up] + cb * pltpu.roll(g, shift, 1)) * inv_main
            h = fpad[k, edge]
            spad[k, edge] = (cc * h + ca * fpad[k, edge_up] + cb * pltpu.roll(h, shift, 1)) * inv_edge

    gather(1)
    gather(0)
    gather(2)

    gathered(0)
    wide = pl.ds(TILE, nx + 2 * TILE)
    u = [jnp.concatenate([uh[0, 0, c], full[0, c], uh[0, 1, c]], axis=0) for c in range(4)]
    rs, ux, uy, temp = physical_variables(u)
    rate = rpad[wide]
    phys[0, wide] = ux
    phys[1, wide] = uy
    phys[2, wide] = -0.5 / temp
    phys[3, wide] = rs / temp * (rate / (1.0 + rate))

    first_row = lax.broadcasted_iota(jnp.int32, (TILE, ny), 0) == 0
    for n in range(4):
        phys[n, pl.ds(0, TILE)] = jnp.where(
            first_row, phys[n, pl.ds(end, TILE)], phys[n, pl.ds(TILE, TILE)]
        )

    @pl.loop(0, 1 + nx // TILE)
    def _(t):
        rows = pl.ds(pl.multiple_of((t + 1) * TILE, TILE), TILE)
        inner = pl.ds(pl.multiple_of(jnp.where(t == 0, 0, (t + 1) * TILE), TILE), TILE)
        ux, uy, scale, amp = [phys[n, inner] for n in range(4)]
        zero = jnp.zeros_like(ux)

        def half_sums(speeds, drift, keep):
            sums = {0: [zero] * 4, 1: [zero] * 4}
            for n, speed in enumerate(speeds):
                d = speed - drift
                e = jnp.exp(d * d * scale)
                if keep:
                    yt[n, rows] = e
                side = sums[int(speed > 0)]
                e1 = speed * e
                e2 = speed * e1
                sums[int(speed > 0)] = [side[0] + e, side[1] + e1, side[2] + e2, side[3] + speed * e2]
            return sums[1], sums[0]

        xp, xm = half_sums([-vel_max + (i + 0.5) * DVX for i in range(NVX)], ux, False)
        yp, ym = half_sums([-vel_max + (j + 0.5) * DVY for j in range(NVY)], uy, True)
        xs = [a + b for a, b in zip(xp, xm)]
        ys = [a + b for a, b in zip(yp, ym)]
        amp = WEIGHT * amp

        def store(n, coef, x, y):
            x = [coef * amp * t for t in x]
            flux[n, rows] = x[0] * y[0]
            flux[n + 1, rows] = x[1] * y[0]
            flux[n + 2, rows] = x[0] * y[1]
            flux[n + 3, rows] = 0.5 * (x[2] * y[0] + x[0] * y[2])

        store(0, 1.0, xs, ys)
        store(4, fine_ratio, xp[1:], ys)
        store(8, -fine_ratio, xm[1:], ys)
        store(12, fine_ratio, xs, yp[1:])
        store(16, -fine_ratio, xs, ym[1:])

    for c in range(4):
        flux[8 + c, pl.ds(end, TILE)] = flux[8 + c, pl.ds(TILE, TILE)]
    gathered(2)
    below, above = pl.ds(2 * TILE - 1, nx), pl.ds(2 * TILE + 1, nx)
    for c in range(4):
        to_y, from_y = flux[12 + c, main], flux[16 + c, main]
        e_out[c] = full[2, c] + (
            flux[c, main] - flux[4 + c, main] - flux[8 + c, main] - to_y - from_y
            + flux[4 + c, below] + flux[8 + c, above]
            + pltpu.roll(to_y, 1, 1) + pltpu.roll(from_y, ny - 1, 1)
        )
    gathered(1)
    stepped = coarse(full.at[1], uh.at[1])
    for c in range(4):
        delta[c] = e_out[c] - stepped[c]

    def onward(n):
        return [
            remote(corr, vfull, win_send.at[0], win_recv.at[0], (n, v, s)),
            remote(corr.at[:, pl.ds(0, TILE)], vh.at[1], win_send.at[1], win_recv.at[1], (n, v, other)),
            remote(corr.at[:, pl.ds(nx - TILE, TILE)], vh.at[0], win_send.at[2], win_recv.at[2], (n, v, other)),
        ]

    def pass_on():
        @pl.when(w + 1 < nw)
        def _():
            for copy in onward(w + 1):
                copy.start()

    @pl.when(w == 0)
    def _():
        for c in range(4):
            corr[c] = stepped[c] + delta[c]
        pass_on()

    @pl.loop(0, chunks)
    def _(c):
        vx, vy0, half, j0 = chunk_of(first, c)
        shift = ny - 1 - (ny - 2) * half
        ca = fine_ratio * jnp.abs(vx)
        dm = vx - phys[0, main]
        xm = phys[3, main] * jnp.exp(dm * dm * phys[2, main])
        de = vx - phys[0, edge]
        xe = phys[3, edge] * jnp.exp(de * de * phys[2, edge])
        for jj in range(HALF):
            k = c * HALF + jj
            fpad[k, main] = spad[k, main] + xm * yt[j0 + jj, main]
            fpad[k, edge] = spad[k, edge] + xe * yt[j0 + jj, pl.ds(TILE, TILE)]
        for jj in range(HALF):
            k = c * HALF + jj
            cb = fine_ratio * jnp.abs(vy0 + jj * DVY)
            g = fpad[k, main]
            star2[k] = (1.0 - ca - cb) * g + ca * fpad[k, up] + cb * pltpu.roll(g, shift, 1)

    @pl.when(w > 0)
    def _():
        for copy in onward(w):
            copy.wait_recv()
        stepped_on = coarse(vfull, vh)
        for c in range(4):
            corr[c] = stepped_on[c] + delta[c]
        pass_on()

    corr_out[...] = corr[...]

    @pl.when(w + 1 < nw)
    def _():
        for copy in onward(w + 1):
            copy.wait_send()

    for ph in range(3):
        if owners == nv:
            settle(red_in.at[ph], rs_send.at[ph])
            settle(red_in.at[ph], ag_send.at[ph])
        else:
            for d in range(1, nv):
                @pl.when(peer(d) < owners)
                def _():
                    settle(red_in.at[ph, 0], rs_send.at[ph])

            def sent():
                settle(red_in.at[ph], ag_send.at[ph])

            pl.when(v < owners)(sent)

    def edges():
        row = (v * band) % nx
        for ph in range(2):
            for side, at_edge in ((0, row == 0), (1, row + band == nx)):
                @pl.when(at_edge)
                def _():
                    for _ in range(nv):
                        settle(uh.at[ph, 0, 0], edge_send.at[2 * ph + side])

    owner(edges)


def lift_kernel(parts, star2, corr, ending, r, lifted, corrected, ye, yc, out, save_sem):
    count = star2.shape[0]
    first = lax.axis_index("vel") * count
    corrected[...] = corr[...]
    inv = 1.0 / (1.0 + r[...])
    sides = []
    for u, table in ((ending, ye), (corr, yc)):
        rs, ux, uy, temp = physical_variables(u)
        scale = -0.5 / temp
        amp = rs / temp
        sides.append((ux, scale, amp))
        for j in range(NVY):
            d = (-vel_max + (j + 0.5) * DVY) - uy
            table[j] = jnp.exp(d * d * scale)
    (ue, se, me), (uc, sc, mc) = sides
    me = me * inv
    chunks = count // HALF
    per = chunks // parts

    def save(n):
        rows = pl.ds(n * per * HALF, per * HALF)
        return pltpu.make_async_copy(out.at[rows], lifted.at[rows], save_sem.at[n])

    for n in range(parts):

        @pl.loop(n * per, (n + 1) * per)
        def _(c):
            vx, _vy, _half, j0 = chunk_of(first, c)
            de, dc = vx - ue, vx - uc
            xe = me * jnp.exp(de * de * se)
            xc = mc * jnp.exp(dc * dc * sc)
            for jj in range(HALF):
                k = c * HALF + jj
                out[k] = star2[k] * inv - xe * ye[j0 + jj] + xc * yc[j0 + jj]

        save(n).start()
    for n in range(parts):
        save(n).wait()


def per_device(nw, nv, f_start, relax_rate):
    field = f_start[0]
    count, nx, ny = field.shape
    owners = min(nv, 4 * nx // TILE)
    band = 4 * nx // owners
    pad = nx + 4 * TILE
    vmem = pltpu.VMEM
    dma = pltpu.SemaphoreType.DMA
    small = jax.ShapeDtypeStruct((4, nx, ny), f32)
    in_vmem = pl.BlockSpec(memory_space=pltpu.VMEM)
    in_hbm = pl.BlockSpec(memory_space=pltpu.HBM)
    field = pltpu.with_memory_space_constraint(field, pltpu.HBM)
    star2, corr, ending = pl.pallas_call(
        functools.partial(advance_kernel, nw, nv, owners),
        out_shape=(jax.ShapeDtypeStruct((count, nx, ny), f32), small, small),
        in_specs=[in_hbm, in_hbm],
        out_specs=(in_vmem, in_vmem, in_vmem),
        scratch_shapes=[
            vmem((count, pad, ny), f32),
            vmem((count, pad, ny), f32),
            vmem((pad, ny), f32),
            vmem((2, len(ORDERS), pad, ny), f32),
            vmem((2, len(ORDERS), pad, ny), f32),
            vmem((3, 4, nx, ny), f32),
            vmem((3, nv - 1, band, ny), f32),
            vmem((3, 4, nx, ny), f32),
            vmem((2, 2, 4, TILE, ny), f32),
            vmem((4, nx, ny), f32),
            vmem((2, 4, TILE, ny), f32),
            vmem((4, nx, ny), f32),
            vmem((NVY, pad, ny), f32),
            vmem((20, pad, ny), f32),
            vmem((4, pad, ny), f32),
            vmem((4, nx, ny), f32),
            dma((2,)), dma((4,)), dma((4,)), dma((3,)), dma((3,)), dma((3,)), dma((3,)),
            dma((4,)), dma((2,)), dma((3,)), dma((3,)),
        ],
        compiler_params=pltpu.CompilerParams(
            collective_id=0, has_side_effects=True, vmem_limit_bytes=40 << 20
        ),
        name="advance",
    )(field, pltpu.with_memory_space_constraint(relax_rate, pltpu.HBM))

    chunks = count // HALF
    parts = next(n for n in (6, 4, 3, 2, 1) if chunks % n == 0)
    lifted, corrected = pl.pallas_call(
        functools.partial(lift_kernel, parts),
        out_shape=(jax.ShapeDtypeStruct((count, nx, ny), f32), small),
        in_specs=[in_vmem] * 4,
        out_specs=(in_hbm, in_vmem),
        scratch_shapes=[
            vmem((NVY, nx, ny), f32), vmem((NVY, nx, ny), f32), vmem((count, nx, ny), f32), dma((parts,)),
        ],
        compiler_params=pltpu.CompilerParams(vmem_limit_bytes=16 << 20),
        name="lift",
    )(star2, corr, ending, relax_rate)
    return corrected[None], lifted[None]


def solution(mesh):
    return jax.shard_map(
        functools.partial(per_device, mesh.shape["win"], mesh.shape["vel"]),
        mesh=mesh,
        in_specs=(P("win", "vel", "sp", None), P("sp", None)),
        out_specs=(P("win", None, "sp", None), P("win", "vel", "sp", None)),
        check_vma=False,
    )
```

```python
import functools
import math

import jax
import jax.numpy as jnp
from jax import lax
from jax.experimental import pallas as pl
from jax.experimental.pallas import tpu as pltpu
from jax.sharding import PartitionSpec as P

NVX = 48
NVY = 32
HALF = NVY // 2
TILE = 8
vel_max = 6.0
fine_ratio = 0.075
coarse_ratio = 0.15
density_floor = 0.3
thermal_lower_bound = 0.3
DVX = 2.0 * vel_max / NVX
DVY = 2.0 * vel_max / NVY
WEIGHT = DVX * DVY / (2.0 * math.pi)
MESH = pl.DeviceIdType.MESH
f32 = jnp.float32
ORDERS = [(p, q) for p in range(5) for q in range(5 - p)]
PLACE = {order: n for n, order in enumerate(ORDERS)}


def physical_variables(u):
    rs = jnp.maximum(u[0], density_floor)
    ux = u[1] / rs
    uy = u[2] / rs
    temp = jnp.maximum((u[3] - 0.5 * (u[1] * ux + u[2] * uy)) / rs, thermal_lower_bound)
    return rs, ux, uy, temp


def chunk_of(first, c):
    k = first + c * HALF
    i = k // NVY
    j = k % NVY
    vx = -vel_max + (i.astype(f32) + 0.5) * DVX
    vy = -vel_max + (j.astype(f32) + 0.5) * DVY
    return vx, vy, j // HALF, j


def framed(main, above, below):
    tile = (TILE, main.shape[1])
    return jnp.concatenate(
        [jnp.broadcast_to(above, tile), main, jnp.broadcast_to(below, tile)], axis=0
    )


def coarse(main, halo):
    nx = main.shape[1]
    rows = nx + 2 * TILE
    ny = main.shape[2]
    u = [framed(main[c], halo[0, c], halo[1, c]) for c in range(4)]
    rs, ux, uy, temp = physical_variables(u)
    p = rs * temp
    wave = jnp.sqrt(2.0 * temp)
    fx = [u[1], u[1] * ux + p, u[2] * ux, (u[3] + p) * ux]
    fy = [u[2], u[1] * uy, u[2] * uy + p, (u[3] + p) * uy]
    sx = jnp.abs(ux) + wave
    sy = jnp.abs(uy) + wave
    mx = jnp.maximum(sx, pltpu.roll(sx, rows - 1, 0))
    my = jnp.maximum(sy, pltpu.roll(sy, ny - 1, 1))
    out = []
    for c in range(4):
        face_x = 0.5 * (fx[c] + pltpu.roll(fx[c], rows - 1, 0)) - 0.5 * mx * (
            pltpu.roll(u[c], rows - 1, 0) - u[c]
        )
        face_y = 0.5 * (fy[c] + pltpu.roll(fy[c], ny - 1, 1)) - 0.5 * my * (
            pltpu.roll(u[c], ny - 1, 1) - u[c]
        )
        g = u[c] - coarse_ratio * (
            face_x - pltpu.roll(face_x, 1, 0) + (face_y - pltpu.roll(face_y, 1, 1))
        )
        out.append(g[TILE : TILE + nx])
    return out


def advance_kernel(
    nw, nv, owners,
    f, r, star2, corr_out,
    fpad, spad, rpad, bsum, hsum, part, red_in, full, uh, edge_rows, vfull, vh, corr, corr_rows, e_out, ye, yt, flux, phys, delta,
    load_sem, halo_send, halo_recv, rs_send, rs_recv, ag_send, ag_recv, edge_send, edge_recv,
    win_send, win_recv,
):
    w, v, s = lax.axis_index("win"), lax.axis_index("vel"), lax.axis_index("sp")
    count, nx, ny = f.shape
    chunks = count // HALF
    first = v * count
    other = 1 - s
    pos = (2 * v) // nv
    main = pl.ds(2 * TILE, nx)
    end = 2 * TILE + nx
    up = pl.ds(2 * TILE + 1 - 2 * pos, nx)
    hb = pl.multiple_of(end - (end - TILE) * pos, TILE)
    edge = pl.ds(hb, TILE)
    edge_up = pl.ds(hb + 1 - 2 * pos, TILE)
    band = 4 * nx // owners

    def peer(d):
        return lax.rem(v + d, nv)

    load_f = pltpu.make_async_copy(f, fpad.at[:, main], load_sem.at[0])
    load_r = pltpu.make_async_copy(r, rpad.at[main], load_sem.at[1])
    load_f.start()
    load_r.start()

    barrier = pltpu.get_barrier_semaphore()
    for d in range(1, nv):
        pl.semaphore_signal(barrier, inc=1, device_id=(w, peer(d), s), device_id_type=MESH)
    for d in range(nv):
        pl.semaphore_signal(barrier, inc=1, device_id=(w, peer(d), other), device_id_type=MESH)

    @pl.when(w + 1 < nw)
    def _():
        pl.semaphore_signal(barrier, inc=1, device_id=(w + 1, v, s), device_id_type=MESH)
        pl.semaphore_signal(barrier, inc=1, device_id=(w + 1, v, other), device_id_type=MESH)

    @pl.when(w > 0)
    def _():
        pl.semaphore_signal(barrier, inc=1, device_id=(w - 1, v, s), device_id_type=MESH)
        pl.semaphore_signal(barrier, inc=1, device_id=(w - 1, v, other), device_id_type=MESH)

    def remote(src, dst, send, recv, device):
        return pltpu.make_async_remote_copy(
            src_ref=src, dst_ref=dst, send_sem=send, recv_sem=recv,
            device_id=device, device_id_type=MESH,
        )

    def band_of(o):
        row = o * band
        return row // nx, pl.ds(pl.multiple_of(row % nx, TILE), band)

    def scatter(ph):
        for d in range(1, nv):
            def send(d=d):
                comp, rows = band_of(peer(d))
                remote(
                    part.at[ph, comp, rows], red_in.at[ph, d - 1], rs_send.at[ph], rs_recv.at[ph],
                    (w, peer(d), s),
                ).start()

            if owners == nv:
                send()
            else:
                pl.when(peer(d) < owners)(send)

    def owner(fn):
        if owners == nv:
            fn()
        else:
            pl.when(v < owners)(fn)

    def settle(ref, sem):
        pltpu.make_async_copy(ref, ref, sem).wait()

    def gather(ph):
        def go():
            settle(red_in.at[ph], rs_recv.at[ph])
            comp, rows = band_of(v)
            total = part[ph, comp, rows]
            for d in range(1, nv):
                total = total + red_in[ph, d - 1]
            full[ph, comp, rows] = total
            for d in range(1, nv):
                remote(
                    full.at[ph, comp, rows], full.at[ph, comp, rows], ag_send.at[ph], ag_recv.at[ph],
                    (w, peer(d), s),
                ).start()
            if ph < 2:
                row = (v * band) % nx
                edge_rows[ph, 0] = total[:1]
                edge_rows[ph, 1] = total[-1:]

                @pl.when(row == 0)
                def _():
                    for d in range(nv):
                        remote(
                            edge_rows.at[ph, 0], uh.at[ph, 1, comp],
                            edge_send.at[2 * ph], edge_recv.at[ph], (w, peer(d), other),
                        ).start()

                @pl.when(row + band == nx)
                def _():
                    for d in range(nv):
                        remote(
                            edge_rows.at[ph, 1], uh.at[ph, 0, comp],
                            edge_send.at[2 * ph + 1], edge_recv.at[ph], (w, peer(d), other),
                        ).start()

        owner(go)

    def gathered(ph):
        def mine():
            for _ in range(owners - 1):
                settle(red_in.at[ph, 0], ag_recv.at[ph])

        def all_of_them():
            for _ in range(owners):
                settle(red_in.at[ph, 0], ag_recv.at[ph])

        if owners == nv:
            settle(red_in.at[ph], ag_recv.at[ph])
        else:
            pl.when(v < owners)(mine)
            pl.when(v >= owners)(all_of_them)
        if ph < 2:
            settle(uh.at[ph], edge_recv.at[ph])

    load_f.wait()
    parity = (first // HALF) % 2
    rounds = (chunks + 1) // 2

    @pl.loop(0, nx // TILE)
    def _(t):
        rows = pl.ds(pl.multiple_of(2 * TILE + t * TILE, TILE), TILE)
        for h in range(2):
            acc = {order: jnp.zeros((TILE, ny), f32) for order in ORDERS}
            for n in range(rounds):
                c = (h + parity) % 2 + 2 * n
                weight = 1.0
                if chunks % 2:
                    weight = jnp.where(c < chunks, 1.0, 0.0).astype(f32)
                    c = jnp.minimum(c, chunks - 1)
                vx = chunk_of(first, c)[0]
                sums = [jnp.zeros((TILE, ny), f32)] * 5
                for jj in range(HALF // 2, HALF):
                    tt = (jj + 0.5) * DVY - 0.5 * vel_max
                    high = fpad[c * HALF + jj, rows]
                    low = fpad[c * HALF + HALF - 1 - jj, rows]
                    even, odd = high + low, high - low
                    sums = [
                        sums[0] + even, sums[1] + tt * odd, sums[2] + tt**2 * even,
                        sums[3] + tt**3 * odd, sums[4] + tt**4 * even,
                    ]
                power = weight
                for q in range(5):
                    for m in range(5 - q):
                        term = sums[m] if q == 0 and chunks % 2 == 0 else sums[m] * power
                        acc[m, q] = acc[m, q] + term
                    power = power * vx
            centre = (h - 0.5) * vel_max
            for p, q in ORDERS:
                total = acc[p, q]
                for m in range(p):
                    total = total + (math.comb(p, m) * centre ** (p - m)) * acc[m, q]
                bsum[h, PLACE[p, q], rows] = total

    def components(ph, get):
        part[ph, 0] = WEIGHT * get(0, 0)
        part[ph, 1] = WEIGHT * get(0, 1)
        part[ph, 2] = WEIGHT * get(1, 0)
        part[ph, 3] = (0.5 * WEIGHT) * (get(0, 2) + get(2, 0))

    components(1, lambda p, q: bsum[0, PLACE[p, q], main] + bsum[1, PLACE[p, q], main])

    ends = jnp.where(w > 0, 2, 0) + jnp.where(w + 1 < nw, 2, 0)
    pl.semaphore_wait(barrier, 2 * nv - 1 + ends)
    load_r.wait()

    source = pl.ds(pl.multiple_of((nx - TILE) * pos, TILE), TILE)
    kept = pl.ds(pl.multiple_of(2 * TILE + (nx - TILE) * pos, TILE), TILE)
    halos = [
        remote(bsum.at[:, :, kept], bsum.at[:, :, edge], halo_send.at[3], halo_recv.at[3], (w, v, other)),
        remote(r.at[pl.ds(0, TILE)], rpad.at[pl.ds(end, TILE)], halo_send.at[1], halo_recv.at[1], (w, v, other)),
        remote(r.at[pl.ds(nx - TILE, TILE)], rpad.at[pl.ds(TILE, TILE)], halo_send.at[2], halo_recv.at[2], (w, v, other)),
        remote(f.at[:, source], fpad.at[:, edge], halo_send.at[0], halo_recv.at[0], (w, v, other)),
    ]
    for copy in halos:
        copy.start()
    scatter(1)
    for copy in halos[:3]:
        copy.wait()

    inv_main = 1.0 / (1.0 + rpad[main])
    inv_edge = 1.0 / (1.0 + rpad[edge])
    along = fine_ratio * (2 * pos - 1).astype(f32)
    ACROSS = ((-fine_ratio, ny - 1), (fine_ratio, 1))
    MAIN = [(0, 0), (0, 1), (1, 0), (0, 2), (2, 0)]

    def moved(table, h, p, q, rows, rows_up):
        across, shift = ACROSS[h]
        bx = table[h, PLACE[p, q + 1], rows]
        by = table[h, PLACE[p + 1, q], rows]
        return (
            table[h, PLACE[p, q], rows]
            + along * (table[h, PLACE[p, q + 1], rows_up] - bx)
            + across * (pltpu.roll(by, shift, 1) - by)
        )

    first_star = {}
    for h in range(2):
        for p, q in ORDERS:
            if p + q < 4:
                star = moved(bsum, h, p, q, main, up)
                if (p, q) in MAIN:
                    first_star[p, q] = star + first_star[p, q] if h else star
                hsum[h, PLACE[p, q], main] = star * inv_main
        for p, q in MAIN:
            hsum[h, PLACE[p, q + 1], edge] = moved(bsum, h, p, q + 1, edge, edge_up) * inv_edge
    components(0, lambda p, q: first_star[p, q])
    scatter(0)
    again = {
        order: moved(hsum, 0, *order, main, up) + moved(hsum, 1, *order, main, up) for order in MAIN
    }
    components(2, lambda p, q: again[p, q])
    scatter(2)

    halos[3].wait()

    @pl.loop(0, chunks)
    def _(c):
        vx, vy0, half, _j = chunk_of(first, c)
        shift = ny - 1 - (ny - 2) * half
        ca = fine_ratio * jnp.abs(vx)
        for jj in range(HALF):
            k = c * HALF + jj
            cb = fine_ratio * jnp.abs(vy0 + jj * DVY)
            cc = 1.0 - ca - cb
            g = fpad[k, main]
            spad[k, main] = (cc * g + ca * fpad[k, up] + cb * pltpu.roll(g, shift, 1)) * inv_main
            h = fpad[k, edge]
            spad[k, edge] = (cc * h + ca * fpad[k, edge_up] + cb * pltpu.roll(h, shift, 1)) * inv_edge

    gather(1)
    gather(0)
    gather(2)

    gathered(1)
    stepped = coarse(full.at[1], uh.at[1])
    for c in range(4):
        delta[c] = stepped[c]
    gathered(0)
    wide = pl.ds(TILE, nx + 2 * TILE)
    u = [framed(full[0, c], uh[0, 0, c], uh[0, 1, c]) for c in range(4)]
    rs, ux, uy, temp = physical_variables(u)
    rate = rpad[wide]
    phys[0, wide] = ux
    phys[1, wide] = uy
    phys[2, wide] = -0.5 / temp
    phys[3, wide] = rs / temp * (rate / (1.0 + rate))

    first_row = lax.broadcasted_iota(jnp.int32, (TILE, ny), 0) == 0
    for n in range(4):
        phys[n, pl.ds(0, TILE)] = jnp.where(
            first_row, phys[n, pl.ds(end, TILE)], phys[n, pl.ds(TILE, TILE)]
        )

    @pl.loop(0, 1 + nx // TILE)
    def _(t):
        rows = pl.ds(pl.multiple_of((t + 1) * TILE, TILE), TILE)
        inner = pl.ds(pl.multiple_of(jnp.where(t == 0, 0, (t + 1) * TILE), TILE), TILE)
        ux, uy, scale, amp = [phys[n, inner] for n in range(4)]
        zero = jnp.zeros_like(ux)

        def half_sums(speeds, drift, keep):
            sums = {0: [zero] * 4, 1: [zero] * 4}
            for n, speed in enumerate(speeds):
                d = speed - drift
                e = jnp.exp(d * d * scale)
                if keep:
                    yt[n, rows] = e
                side = sums[int(speed > 0)]
                e1 = speed * e
                e2 = speed * e1
                sums[int(speed > 0)] = [side[0] + e, side[1] + e1, side[2] + e2, side[3] + speed * e2]
            return sums[1], sums[0]

        xp, xm = half_sums([-vel_max + (i + 0.5) * DVX for i in range(NVX)], ux, False)
        yp, ym = half_sums([-vel_max + (j + 0.5) * DVY for j in range(NVY)], uy, True)
        xs = [a + b for a, b in zip(xp, xm)]
        ys = [a + b for a, b in zip(yp, ym)]
        amp = WEIGHT * amp

        def store(n, coef, x, y):
            x = [coef * amp * t for t in x]
            flux[n, rows] = x[0] * y[0]
            flux[n + 1, rows] = x[1] * y[0]
            flux[n + 2, rows] = x[0] * y[1]
            flux[n + 3, rows] = 0.5 * (x[2] * y[0] + x[0] * y[2])

        store(0, 1.0, xs, ys)
        store(4, fine_ratio, xp[1:], ys)
        store(8, -fine_ratio, xm[1:], ys)
        store(12, fine_ratio, xs, yp[1:])
        store(16, -fine_ratio, xs, ym[1:])

    for c in range(4):
        flux[8 + c, pl.ds(end, TILE)] = flux[8 + c, pl.ds(TILE, TILE)]
    gathered(2)
    below, above = pl.ds(2 * TILE - 1, nx), pl.ds(2 * TILE + 1, nx)
    for c in range(4):
        to_y, from_y = flux[12 + c, main], flux[16 + c, main]
        e_out[c] = full[2, c] + (
            flux[c, main] - flux[4 + c, main] - flux[8 + c, main] - to_y - from_y
            + flux[4 + c, below] + flux[8 + c, above]
            + pltpu.roll(to_y, 1, 1) + pltpu.roll(from_y, ny - 1, 1)
        )
    for c in range(4):
        start_step = delta[c]
        delta[c] = e_out[c] - start_step
        corr[c] = start_step

    def onward(n):
        return [
            remote(corr, vfull, win_send.at[0], win_recv.at[0], (n, v, s)),
            remote(corr_rows.at[0], vh.at[1], win_send.at[1], win_recv.at[1], (n, v, other)),
            remote(corr_rows.at[1], vh.at[0], win_send.at[2], win_recv.at[2], (n, v, other)),
        ]

    def store_corrected(c, value):
        corr[c] = value
        corr_rows[0, c] = value[:1]
        corr_rows[1, c] = value[-1:]

    def pass_on():
        @pl.when(w + 1 < nw)
        def _():
            for copy in onward(w + 1):
                copy.start()

    @pl.when(w == 0)
    def _():
        for c in range(4):
            store_corrected(c, corr[c] + delta[c])
        pass_on()

    rs, ux, uy, temp = physical_variables(e_out)
    scale = -0.5 / temp
    phys[4, main] = ux
    phys[5, main] = scale
    phys[6, main] = rs / temp * inv_main
    for j in range(NVY):
        d = (-vel_max + (j + 0.5) * DVY) - uy
        ye[j] = jnp.exp(d * d * scale)

    @pl.loop(0, chunks)
    def _(c):
        vx, vy0, half, j0 = chunk_of(first, c)
        shift = ny - 1 - (ny - 2) * half
        ca = fine_ratio * jnp.abs(vx)
        dm = vx - phys[0, main]
        xm = phys[3, main] * jnp.exp(dm * dm * phys[2, main])
        de = vx - phys[0, edge]
        dn = vx - phys[4, main]
        x_end = phys[6, main] * jnp.exp(dn * dn * phys[5, main])
        xe = phys[3, edge] * jnp.exp(de * de * phys[2, edge])
        for jj in range(HALF):
            k = c * HALF + jj
            fpad[k, main] = spad[k, main] + xm * yt[j0 + jj, main]
            fpad[k, edge] = spad[k, edge] + xe * yt[j0 + jj, pl.ds(TILE, TILE)]
        for jj in range(HALF):
            k = c * HALF + jj
            cb = fine_ratio * jnp.abs(vy0 + jj * DVY)
            g = fpad[k, main]
            star = (1.0 - ca - cb) * g + ca * fpad[k, up] + cb * pltpu.roll(g, shift, 1)
            star2[k] = star * inv_main - x_end * ye[j0 + jj]

    @pl.when(w > 0)
    def _():
        for copy in onward(w):
            copy.wait_recv()
        stepped_on = coarse(vfull, vh)
        for c in range(4):
            store_corrected(c, stepped_on[c] + delta[c])
        pass_on()

    corr_out[...] = corr[...]

    @pl.when(w + 1 < nw)
    def _():
        for copy in onward(w + 1):
            copy.wait_send()

    for ph in range(3):
        if owners == nv:
            settle(red_in.at[ph], rs_send.at[ph])
            settle(red_in.at[ph], ag_send.at[ph])
        else:
            for d in range(1, nv):
                @pl.when(peer(d) < owners)
                def _():
                    settle(red_in.at[ph, 0], rs_send.at[ph])

            def sent():
                settle(red_in.at[ph], ag_send.at[ph])

            pl.when(v < owners)(sent)

    def edges():
        row = (v * band) % nx
        for ph in range(2):
            for side, at_edge in ((0, row == 0), (1, row + band == nx)):
                @pl.when(at_edge)
                def _():
                    for _ in range(nv):
                        settle(uh.at[ph, 0, 0], edge_send.at[2 * ph + side])

    owner(edges)


def lift_kernel(parts, star2, corr, lifted, corrected, yc, out, save_sem):
    count = star2.shape[0]
    first = lax.axis_index("vel") * count
    corrected[...] = corr[...]
    rs, uc, uy, temp = physical_variables(corr)
    sc = -0.5 / temp
    mc = rs / temp
    for j in range(NVY):
        d = (-vel_max + (j + 0.5) * DVY) - uy
        yc[j] = jnp.exp(d * d * sc)
    chunks = count // HALF
    per = chunks // parts

    def save(n):
        rows = pl.ds(n * per * HALF, per * HALF)
        return pltpu.make_async_copy(out.at[rows], lifted.at[rows], save_sem.at[n])

    for n in range(parts):

        @pl.loop(n * per, (n + 1) * per)
        def _(c):
            vx, _vy, _half, j0 = chunk_of(first, c)
            dc = vx - uc
            xc = mc * jnp.exp(dc * dc * sc)
            for jj in range(HALF):
                k = c * HALF + jj
                out[k] = star2[k] + xc * yc[j0 + jj]

        save(n).start()
    for n in range(parts):
        save(n).wait()


def per_device(nw, nv, f_start, relax_rate):
    field = f_start[0]
    count, nx, ny = field.shape
    owners = min(nv, 4 * nx // TILE)
    band = 4 * nx // owners
    pad = nx + 4 * TILE
    vmem = pltpu.VMEM
    dma = pltpu.SemaphoreType.DMA
    small = jax.ShapeDtypeStruct((4, nx, ny), f32)
    in_vmem = pl.BlockSpec(memory_space=pltpu.VMEM)
    in_hbm = pl.BlockSpec(memory_space=pltpu.HBM)
    field = pltpu.with_memory_space_constraint(field, pltpu.HBM)
    star2, corr = pl.pallas_call(
        functools.partial(advance_kernel, nw, nv, owners),
        out_shape=(jax.ShapeDtypeStruct((count, nx, ny), f32), small),
        in_specs=[in_hbm, in_hbm],
        out_specs=(in_vmem, in_vmem),
        scratch_shapes=[
            vmem((count, pad, ny), f32),
            vmem((count, pad, ny), f32),
            vmem((pad, ny), f32),
            vmem((2, len(ORDERS), pad, ny), f32),
            vmem((2, len(ORDERS), pad, ny), f32),
            vmem((3, 4, nx, ny), f32),
            vmem((3, nv - 1, band, ny), f32),
            vmem((3, 4, nx, ny), f32),
            vmem((2, 2, 4, 1, ny), f32),
            vmem((2, 2, 1, ny), f32),
            vmem((4, nx, ny), f32),
            vmem((2, 4, 1, ny), f32),
            vmem((4, nx, ny), f32),
            vmem((2, 4, 1, ny), f32),
            vmem((4, nx, ny), f32),
            vmem((NVY, nx, ny), f32),
            vmem((NVY, pad, ny), f32),
            vmem((20, pad, ny), f32),
            vmem((7, pad, ny), f32),
            vmem((4, nx, ny), f32),
            dma((2,)), dma((4,)), dma((4,)), dma((3,)), dma((3,)), dma((3,)), dma((3,)),
            dma((4,)), dma((2,)), dma((3,)), dma((3,)),
        ],
        compiler_params=pltpu.CompilerParams(
            collective_id=0, has_side_effects=True, vmem_limit_bytes=40 << 20
        ),
        name="advance",
    )(field, pltpu.with_memory_space_constraint(relax_rate, pltpu.HBM))

    chunks = count // HALF
    parts = next(n for n in (6, 4, 3, 2, 1) if chunks % n == 0)
    lifted, corrected = pl.pallas_call(
        functools.partial(lift_kernel, parts),
        out_shape=(jax.ShapeDtypeStruct((count, nx, ny), f32), small),
        in_specs=[in_vmem] * 2,
        out_specs=(in_hbm, in_vmem),
        scratch_shapes=[
            vmem((NVY, nx, ny), f32), vmem((count, nx, ny), f32), dma((parts,)),
        ],
        compiler_params=pltpu.CompilerParams(vmem_limit_bytes=16 << 20),
        name="lift",
    )(star2, corr)
    return corrected[None], lifted[None]


def solution(mesh):
    return jax.shard_map(
        functools.partial(per_device, mesh.shape["win"], mesh.shape["vel"]),
        mesh=mesh,
        in_specs=(P("win", "vel", "sp", None), P("sp", None)),
        out_specs=(P("win", None, "sp", None), P("win", "vel", "sp", None)),
        check_vma=False,
    )
```

```python
import functools
import math

import jax
import jax.numpy as jnp
from jax import lax
from jax.experimental import pallas as pl
from jax.experimental.pallas import tpu as pltpu
from jax.sharding import PartitionSpec as P

NVX = 48
NVY = 32
HALF = NVY // 2
TILE = 8
vel_max = 6.0
fine_ratio = 0.075
coarse_ratio = 0.15
density_floor = 0.3
thermal_lower_bound = 0.3
DVX = 2.0 * vel_max / NVX
DVY = 2.0 * vel_max / NVY
WEIGHT = DVX * DVY / (2.0 * math.pi)
MESH = pl.DeviceIdType.MESH
f32 = jnp.float32
ORDERS = [(p, q) for p in range(5) for q in range(5 - p)]
PLACE = {order: n for n, order in enumerate(ORDERS)}


def physical_variables(u):
    rs = jnp.maximum(u[0], density_floor)
    ux = u[1] / rs
    uy = u[2] / rs
    temp = jnp.maximum((u[3] - 0.5 * (u[1] * ux + u[2] * uy)) / rs, thermal_lower_bound)
    return rs, ux, uy, temp


def chunk_of(first, c):
    k = first + c * HALF
    i = k // NVY
    j = k % NVY
    vx = -vel_max + (i.astype(f32) + 0.5) * DVX
    vy = -vel_max + (j.astype(f32) + 0.5) * DVY
    return vx, vy, j // HALF, j


def framed(main, above, below):
    tile = (TILE, main.shape[1])
    return jnp.concatenate(
        [jnp.broadcast_to(above, tile), main, jnp.broadcast_to(below, tile)], axis=0
    )


def coarse(main, halo):
    nx = main.shape[1]
    rows = nx + 2 * TILE
    ny = main.shape[2]
    u = [framed(main[c], halo[0, c], halo[1, c]) for c in range(4)]
    rs, ux, uy, temp = physical_variables(u)
    p = rs * temp
    wave = jnp.sqrt(2.0 * temp)
    fx = [u[1], u[1] * ux + p, u[2] * ux, (u[3] + p) * ux]
    fy = [u[2], u[1] * uy, u[2] * uy + p, (u[3] + p) * uy]
    sx = jnp.abs(ux) + wave
    sy = jnp.abs(uy) + wave
    mx = jnp.maximum(sx, pltpu.roll(sx, rows - 1, 0))
    my = jnp.maximum(sy, pltpu.roll(sy, ny - 1, 1))
    out = []
    for c in range(4):
        face_x = 0.5 * (fx[c] + pltpu.roll(fx[c], rows - 1, 0)) - 0.5 * mx * (
            pltpu.roll(u[c], rows - 1, 0) - u[c]
        )
        face_y = 0.5 * (fy[c] + pltpu.roll(fy[c], ny - 1, 1)) - 0.5 * my * (
            pltpu.roll(u[c], ny - 1, 1) - u[c]
        )
        g = u[c] - coarse_ratio * (
            face_x - pltpu.roll(face_x, 1, 0) + (face_y - pltpu.roll(face_y, 1, 1))
        )
        out.append(g[TILE : TILE + nx])
    return out


def advance_kernel(
    nw, nv, owners,
    f, r, star2, corr_out,
    fpad, spad, rpad, bsum, hsum, part, red_in, full, uh, edge_rows, vfull, vh, corr, corr_rows, e_out, ye, yt, flux, phys, delta,
    load_sem, halo_send, halo_recv, rs_send, rs_recv, ag_send, ag_recv, edge_send, edge_recv,
    win_send, win_recv,
):
    w, v, s = lax.axis_index("win"), lax.axis_index("vel"), lax.axis_index("sp")
    count, nx, ny = f.shape
    chunks = count // HALF
    first = v * count
    other = 1 - s
    pos = (2 * v) // nv
    main = pl.ds(2 * TILE, nx)
    end = 2 * TILE + nx
    up = pl.ds(2 * TILE + 1 - 2 * pos, nx)
    hb = pl.multiple_of(end - (end - TILE) * pos, TILE)
    edge = pl.ds(hb, TILE)
    edge_up = pl.ds(hb + 1 - 2 * pos, TILE)
    band = 4 * nx // owners

    def peer(d):
        return lax.rem(v + d, nv)

    tiles = nx // TILE

    def load_f(t):
        rows = pl.ds(pl.multiple_of(t * TILE, TILE), TILE)
        padded = pl.ds(pl.multiple_of((t + 2) * TILE, TILE), TILE)
        return pltpu.make_async_copy(f.at[:, rows], fpad.at[:, padded], load_sem.at[t])

    for t in range(tiles):
        load_f(t).start()
    load_r = pltpu.make_async_copy(r, rpad.at[main], load_sem.at[tiles])
    load_r.start()

    barrier = pltpu.get_barrier_semaphore()
    for d in range(1, nv):
        pl.semaphore_signal(barrier, inc=1, device_id=(w, peer(d), s), device_id_type=MESH)
    for d in range(nv):
        pl.semaphore_signal(barrier, inc=1, device_id=(w, peer(d), other), device_id_type=MESH)

    @pl.when(w + 1 < nw)
    def _():
        pl.semaphore_signal(barrier, inc=1, device_id=(w + 1, v, s), device_id_type=MESH)
        pl.semaphore_signal(barrier, inc=1, device_id=(w + 1, v, other), device_id_type=MESH)

    @pl.when(w > 0)
    def _():
        pl.semaphore_signal(barrier, inc=1, device_id=(w - 1, v, s), device_id_type=MESH)
        pl.semaphore_signal(barrier, inc=1, device_id=(w - 1, v, other), device_id_type=MESH)

    def remote(src, dst, send, recv, device):
        return pltpu.make_async_remote_copy(
            src_ref=src, dst_ref=dst, send_sem=send, recv_sem=recv,
            device_id=device, device_id_type=MESH,
        )

    def band_of(o):
        row = o * band
        return row // nx, pl.ds(pl.multiple_of(row % nx, TILE), band)

    def scatter(ph):
        for d in range(1, nv):
            def send(d=d):
                comp, rows = band_of(peer(d))
                remote(
                    part.at[ph, comp, rows], red_in.at[ph, d - 1], rs_send.at[ph], rs_recv.at[ph],
                    (w, peer(d), s),
                ).start()

            if owners == nv:
                send()
            else:
                pl.when(peer(d) < owners)(send)

    def owner(fn):
        if owners == nv:
            fn()
        else:
            pl.when(v < owners)(fn)

    def settle(ref, sem):
        pltpu.make_async_copy(ref, ref, sem).wait()

    def gather(ph):
        def go():
            settle(red_in.at[ph], rs_recv.at[ph])
            comp, rows = band_of(v)
            total = part[ph, comp, rows]
            for d in range(1, nv):
                total = total + red_in[ph, d - 1]
            full[ph, comp, rows] = total
            for d in range(1, nv):
                remote(
                    full.at[ph, comp, rows], full.at[ph, comp, rows], ag_send.at[ph], ag_recv.at[ph],
                    (w, peer(d), s),
                ).start()
            if ph < 2:
                row = (v * band) % nx
                edge_rows[ph, 0] = total[:1]
                edge_rows[ph, 1] = total[-1:]

                @pl.when(row == 0)
                def _():
                    for d in range(nv):
                        remote(
                            edge_rows.at[ph, 0], uh.at[ph, 1, comp],
                            edge_send.at[2 * ph], edge_recv.at[ph], (w, peer(d), other),
                        ).start()

                @pl.when(row + band == nx)
                def _():
                    for d in range(nv):
                        remote(
                            edge_rows.at[ph, 1], uh.at[ph, 0, comp],
                            edge_send.at[2 * ph + 1], edge_recv.at[ph], (w, peer(d), other),
                        ).start()

        owner(go)

    def gathered(ph):
        def mine():
            for _ in range(owners - 1):
                settle(red_in.at[ph, 0], ag_recv.at[ph])

        def all_of_them():
            for _ in range(owners):
                settle(red_in.at[ph, 0], ag_recv.at[ph])

        if owners == nv:
            settle(red_in.at[ph], ag_recv.at[ph])
        else:
            pl.when(v < owners)(mine)
            pl.when(v >= owners)(all_of_them)
        if ph < 2:
            settle(uh.at[ph], edge_recv.at[ph])

    parity = (first // HALF) % 2
    rounds = (chunks + 1) // 2

    @pl.loop(0, nx // TILE)
    def _(t):
        load_f(t).wait()
        rows = pl.ds(pl.multiple_of(2 * TILE + t * TILE, TILE), TILE)
        for h in range(2):
            acc = {order: jnp.zeros((TILE, ny), f32) for order in ORDERS}
            for n in range(rounds):
                c = (h + parity) % 2 + 2 * n
                weight = 1.0
                if chunks % 2:
                    weight = jnp.where(c < chunks, 1.0, 0.0).astype(f32)
                    c = jnp.minimum(c, chunks - 1)
                vx = chunk_of(first, c)[0]
                sums = [jnp.zeros((TILE, ny), f32)] * 5
                for jj in range(HALF // 2, HALF):
                    tt = (jj + 0.5) * DVY - 0.5 * vel_max
                    high = fpad[c * HALF + jj, rows]
                    low = fpad[c * HALF + HALF - 1 - jj, rows]
                    even, odd = high + low, high - low
                    sums = [
                        sums[0] + even, sums[1] + tt * odd, sums[2] + tt**2 * even,
                        sums[3] + tt**3 * odd, sums[4] + tt**4 * even,
                    ]
                power = weight
                for q in range(5):
                    for m in range(5 - q):
                        term = sums[m] if q == 0 and chunks % 2 == 0 else sums[m] * power
                        acc[m, q] = acc[m, q] + term
                    power = power * vx
            centre = (h - 0.5) * vel_max
            for p, q in ORDERS:
                total = acc[p, q]
                for m in range(p):
                    total = total + (math.comb(p, m) * centre ** (p - m)) * acc[m, q]
                bsum[h, PLACE[p, q], rows] = total

    def components(ph, get):
        part[ph, 0] = WEIGHT * get(0, 0)
        part[ph, 1] = WEIGHT * get(0, 1)
        part[ph, 2] = WEIGHT * get(1, 0)
        part[ph, 3] = (0.5 * WEIGHT) * (get(0, 2) + get(2, 0))

    components(1, lambda p, q: bsum[0, PLACE[p, q], main] + bsum[1, PLACE[p, q], main])

    ends = jnp.where(w > 0, 2, 0) + jnp.where(w + 1 < nw, 2, 0)
    pl.semaphore_wait(barrier, 2 * nv - 1 + ends)
    load_r.wait()

    source = pl.ds(pl.multiple_of((nx - TILE) * pos, TILE), TILE)
    kept = pl.ds(pl.multiple_of(2 * TILE + (nx - TILE) * pos, TILE), TILE)
    halos = [
        remote(bsum.at[:, :, kept], bsum.at[:, :, edge], halo_send.at[3], halo_recv.at[3], (w, v, other)),
        remote(r.at[pl.ds(0, TILE)], rpad.at[pl.ds(end, TILE)], halo_send.at[1], halo_recv.at[1], (w, v, other)),
        remote(r.at[pl.ds(nx - TILE, TILE)], rpad.at[pl.ds(TILE, TILE)], halo_send.at[2], halo_recv.at[2], (w, v, other)),
        remote(f.at[:, source], fpad.at[:, edge], halo_send.at[0], halo_recv.at[0], (w, v, other)),
    ]
    for copy in halos:
        copy.start()
    scatter(1)
    for copy in halos[:3]:
        copy.wait()

    inv_main = 1.0 / (1.0 + rpad[main])
    inv_edge = 1.0 / (1.0 + rpad[edge])
    along = fine_ratio * (2 * pos - 1).astype(f32)
    ACROSS = ((-fine_ratio, ny - 1), (fine_ratio, 1))
    MAIN = [(0, 0), (0, 1), (1, 0), (0, 2), (2, 0)]

    def moved(table, h, p, q, rows, rows_up):
        across, shift = ACROSS[h]
        bx = table[h, PLACE[p, q + 1], rows]
        by = table[h, PLACE[p + 1, q], rows]
        return (
            table[h, PLACE[p, q], rows]
            + along * (table[h, PLACE[p, q + 1], rows_up] - bx)
            + across * (pltpu.roll(by, shift, 1) - by)
        )

    first_star = {}
    for h in range(2):
        for p, q in ORDERS:
            if p + q < 4:
                star = moved(bsum, h, p, q, main, up)
                if (p, q) in MAIN:
                    first_star[p, q] = star + first_star[p, q] if h else star
                hsum[h, PLACE[p, q], main] = star * inv_main
        for p, q in MAIN:
            hsum[h, PLACE[p, q + 1], edge] = moved(bsum, h, p, q + 1, edge, edge_up) * inv_edge
    components(0, lambda p, q: first_star[p, q])
    scatter(0)
    again = {
        order: moved(hsum, 0, *order, main, up) + moved(hsum, 1, *order, main, up) for order in MAIN
    }
    components(2, lambda p, q: again[p, q])
    scatter(2)

    halos[3].wait()

    @pl.loop(0, chunks)
    def _(c):
        vx, vy0, half, _j = chunk_of(first, c)
        shift = ny - 1 - (ny - 2) * half
        ca = fine_ratio * jnp.abs(vx)
        for jj in range(HALF):
            k = c * HALF + jj
            cb = fine_ratio * jnp.abs(vy0 + jj * DVY)
            cc = 1.0 - ca - cb
            g = fpad[k, main]
            spad[k, main] = (cc * g + ca * fpad[k, up] + cb * pltpu.roll(g, shift, 1)) * inv_main
            h = fpad[k, edge]
            spad[k, edge] = (cc * h + ca * fpad[k, edge_up] + cb * pltpu.roll(h, shift, 1)) * inv_edge

    gather(1)
    gather(0)
    gather(2)

    gathered(1)
    stepped = coarse(full.at[1], uh.at[1])
    for c in range(4):
        delta[c] = stepped[c]
    gathered(0)
    wide = pl.ds(TILE, nx + 2 * TILE)
    u = [framed(full[0, c], uh[0, 0, c], uh[0, 1, c]) for c in range(4)]
    rs, ux, uy, temp = physical_variables(u)
    rate = rpad[wide]
    phys[0, wide] = ux
    phys[1, wide] = uy
    phys[2, wide] = -0.5 / temp
    phys[3, wide] = rs / temp * (rate / (1.0 + rate))

    first_row = lax.broadcasted_iota(jnp.int32, (TILE, ny), 0) == 0
    for n in range(4):
        phys[n, pl.ds(0, TILE)] = jnp.where(
            first_row, phys[n, pl.ds(end, TILE)], phys[n, pl.ds(TILE, TILE)]
        )

    @pl.loop(0, 1 + nx // TILE)
    def _(t):
        rows = pl.ds(pl.multiple_of((t + 1) * TILE, TILE), TILE)
        inner = pl.ds(pl.multiple_of(jnp.where(t == 0, 0, (t + 1) * TILE), TILE), TILE)
        ux, uy, scale, amp = [phys[n, inner] for n in range(4)]
        zero = jnp.zeros_like(ux)

        def half_sums(speeds, drift, keep):
            weights = []
            for n, speed in enumerate(speeds):
                d = speed - drift
                e = jnp.exp(d * d * scale)
                if keep:
                    yt[n, rows] = e
                weights.append(e)
            sides = []
            half = len(speeds) // 2
            for at, c in ((half, 0.5 * vel_max), (0, -0.5 * vel_max)):
                m = [zero] * 4
                for n in range(half // 2, half):
                    t = speeds[at + n] - c
                    high, low = weights[at + n], weights[at + half - 1 - n]
                    even, odd = high + low, high - low
                    m = [m[0] + even, m[1] + t * odd, m[2] + t**2 * even, m[3] + t**3 * odd]
                sides.append([
                    m[0],
                    m[1] + c * m[0],
                    m[2] + (2 * c) * m[1] + c**2 * m[0],
                    m[3] + (3 * c) * m[2] + (3 * c**2) * m[1] + c**3 * m[0],
                ])
            return sides

        xp, xm = half_sums([-vel_max + (i + 0.5) * DVX for i in range(NVX)], ux, False)
        yp, ym = half_sums([-vel_max + (j + 0.5) * DVY for j in range(NVY)], uy, True)
        xs = [a + b for a, b in zip(xp, xm)]
        ys = [a + b for a, b in zip(yp, ym)]
        amp = WEIGHT * amp

        def store(n, coef, x, y):
            x = [coef * amp * t for t in x]
            flux[n, rows] = x[0] * y[0]
            flux[n + 1, rows] = x[1] * y[0]
            flux[n + 2, rows] = x[0] * y[1]
            flux[n + 3, rows] = 0.5 * (x[2] * y[0] + x[0] * y[2])

        store(0, 1.0, xs, ys)
        store(4, fine_ratio, xp[1:], ys)
        store(8, -fine_ratio, xm[1:], ys)
        store(12, fine_ratio, xs, yp[1:])
        store(16, -fine_ratio, xs, ym[1:])

    for c in range(4):
        flux[8 + c, pl.ds(end, TILE)] = flux[8 + c, pl.ds(TILE, TILE)]
    gathered(2)
    below, above = pl.ds(2 * TILE - 1, nx), pl.ds(2 * TILE + 1, nx)
    for c in range(4):
        to_y, from_y = flux[12 + c, main], flux[16 + c, main]
        e_out[c] = full[2, c] + (
            flux[c, main] - flux[4 + c, main] - flux[8 + c, main] - to_y - from_y
            + flux[4 + c, below] + flux[8 + c, above]
            + pltpu.roll(to_y, 1, 1) + pltpu.roll(from_y, ny - 1, 1)
        )
    for c in range(4):
        start_step = delta[c]
        delta[c] = e_out[c] - start_step
        corr[c] = start_step

    def onward(n):
        return [
            remote(corr, vfull, win_send.at[0], win_recv.at[0], (n, v, s)),
            remote(corr_rows.at[0], vh.at[1], win_send.at[1], win_recv.at[1], (n, v, other)),
            remote(corr_rows.at[1], vh.at[0], win_send.at[2], win_recv.at[2], (n, v, other)),
        ]

    def store_corrected(c, value):
        corr[c] = value
        corr_rows[0, c] = value[:1]
        corr_rows[1, c] = value[-1:]

    def pass_on():
        @pl.when(w + 1 < nw)
        def _():
            for copy in onward(w + 1):
                copy.start()

    @pl.when(w == 0)
    def _():
        for c in range(4):
            store_corrected(c, corr[c] + delta[c])
        pass_on()

    rs, ux, uy, temp = physical_variables(e_out)
    scale = -0.5 / temp
    phys[4, main] = ux
    phys[5, main] = scale
    phys[6, main] = rs / temp * inv_main
    for j in range(NVY):
        d = (-vel_max + (j + 0.5) * DVY) - uy
        ye[j] = jnp.exp(d * d * scale)

    @pl.loop(0, chunks)
    def _(c):
        vx, vy0, half, j0 = chunk_of(first, c)
        shift = ny - 1 - (ny - 2) * half
        ca = fine_ratio * jnp.abs(vx)
        dm = vx - phys[0, main]
        xm = phys[3, main] * jnp.exp(dm * dm * phys[2, main])
        de = vx - phys[0, edge]
        dn = vx - phys[4, main]
        x_end = phys[6, main] * jnp.exp(dn * dn * phys[5, main])
        xe = phys[3, edge] * jnp.exp(de * de * phys[2, edge])
        for jj in range(HALF):
            k = c * HALF + jj
            fpad[k, main] = spad[k, main] + xm * yt[j0 + jj, main]
            fpad[k, edge] = spad[k, edge] + xe * yt[j0 + jj, pl.ds(TILE, TILE)]
        for jj in range(HALF):
            k = c * HALF + jj
            cb = fine_ratio * jnp.abs(vy0 + jj * DVY)
            g = fpad[k, main]
            star = (1.0 - ca - cb) * g + ca * fpad[k, up] + cb * pltpu.roll(g, shift, 1)
            star2[k] = star * inv_main - x_end * ye[j0 + jj]

    @pl.when(w > 0)
    def _():
        for copy in onward(w):
            copy.wait_recv()
        stepped_on = coarse(vfull, vh)
        for c in range(4):
            store_corrected(c, stepped_on[c] + delta[c])
        pass_on()

    corr_out[...] = corr[...]

    @pl.when(w + 1 < nw)
    def _():
        for copy in onward(w + 1):
            copy.wait_send()

    for ph in range(3):
        if owners == nv:
            settle(red_in.at[ph], rs_send.at[ph])
            settle(red_in.at[ph], ag_send.at[ph])
        else:
            for d in range(1, nv):
                @pl.when(peer(d) < owners)
                def _():
                    settle(red_in.at[ph, 0], rs_send.at[ph])

            def sent():
                settle(red_in.at[ph], ag_send.at[ph])

            pl.when(v < owners)(sent)

    def edges():
        row = (v * band) % nx
        for ph in range(2):
            for side, at_edge in ((0, row == 0), (1, row + band == nx)):
                @pl.when(at_edge)
                def _():
                    for _ in range(nv):
                        settle(uh.at[ph, 0, 0], edge_send.at[2 * ph + side])

    owner(edges)


def lift_kernel(parts, star2, corr, lifted, corrected, yc, out, save_sem):
    count = star2.shape[0]
    first = lax.axis_index("vel") * count
    corrected[...] = corr[...]
    rs, uc, uy, temp = physical_variables(corr)
    sc = -0.5 / temp
    mc = rs / temp
    for j in range(NVY):
        d = (-vel_max + (j + 0.5) * DVY) - uy
        yc[j] = jnp.exp(d * d * sc)
    chunks = count // HALF
    per = chunks // parts

    def save(n):
        rows = pl.ds(n * per * HALF, per * HALF)
        return pltpu.make_async_copy(out.at[rows], lifted.at[rows], save_sem.at[n])

    for n in range(parts):

        @pl.loop(n * per, (n + 1) * per)
        def _(c):
            vx, _vy, _half, j0 = chunk_of(first, c)
            dc = vx - uc
            xc = mc * jnp.exp(dc * dc * sc)
            for jj in range(HALF):
                k = c * HALF + jj
                out[k] = star2[k] + xc * yc[j0 + jj]

        save(n).start()
    for n in range(parts):
        save(n).wait()


def per_device(nw, nv, f_start, relax_rate):
    field = f_start[0]
    count, nx, ny = field.shape
    owners = min(nv, 4 * nx // TILE)
    band = 4 * nx // owners
    pad = nx + 4 * TILE
    vmem = pltpu.VMEM
    dma = pltpu.SemaphoreType.DMA
    small = jax.ShapeDtypeStruct((4, nx, ny), f32)
    in_vmem = pl.BlockSpec(memory_space=pltpu.VMEM)
    in_hbm = pl.BlockSpec(memory_space=pltpu.HBM)
    field = pltpu.with_memory_space_constraint(field, pltpu.HBM)
    star2, corr = pl.pallas_call(
        functools.partial(advance_kernel, nw, nv, owners),
        out_shape=(jax.ShapeDtypeStruct((count, nx, ny), f32), small),
        in_specs=[in_hbm, in_hbm],
        out_specs=(in_vmem, in_vmem),
        scratch_shapes=[
            vmem((count, pad, ny), f32),
            vmem((count, pad, ny), f32),
            vmem((pad, ny), f32),
            vmem((2, len(ORDERS), pad, ny), f32),
            vmem((2, len(ORDERS), pad, ny), f32),
            vmem((3, 4, nx, ny), f32),
            vmem((3, nv - 1, band, ny), f32),
            vmem((3, 4, nx, ny), f32),
            vmem((2, 2, 4, 1, ny), f32),
            vmem((2, 2, 1, ny), f32),
            vmem((4, nx, ny), f32),
            vmem((2, 4, 1, ny), f32),
            vmem((4, nx, ny), f32),
            vmem((2, 4, 1, ny), f32),
            vmem((4, nx, ny), f32),
            vmem((NVY, nx, ny), f32),
            vmem((NVY, pad, ny), f32),
            vmem((20, pad, ny), f32),
            vmem((7, pad, ny), f32),
            vmem((4, nx, ny), f32),
            dma((1 + nx // TILE,)), dma((4,)), dma((4,)), dma((3,)), dma((3,)), dma((3,)), dma((3,)),
            dma((4,)), dma((2,)), dma((3,)), dma((3,)),
        ],
        compiler_params=pltpu.CompilerParams(
            collective_id=0, has_side_effects=True, vmem_limit_bytes=40 << 20
        ),
        name="advance",
    )(field, pltpu.with_memory_space_constraint(relax_rate, pltpu.HBM))

    chunks = count // HALF
    parts = next(n for n in (6, 4, 3, 2, 1) if chunks % n == 0)
    lifted, corrected = pl.pallas_call(
        functools.partial(lift_kernel, parts),
        out_shape=(jax.ShapeDtypeStruct((count, nx, ny), f32), small),
        in_specs=[in_vmem] * 2,
        out_specs=(in_hbm, in_vmem),
        scratch_shapes=[
            vmem((NVY, nx, ny), f32), vmem((count, nx, ny), f32), dma((parts,)),
        ],
        compiler_params=pltpu.CompilerParams(vmem_limit_bytes=16 << 20),
        name="lift",
    )(star2, corr)
    return corrected[None], lifted[None]


def solution(mesh):
    return jax.shard_map(
        functools.partial(per_device, mesh.shape["win"], mesh.shape["vel"]),
        mesh=mesh,
        in_specs=(P("win", "vel", "sp", None), P("sp", None)),
        out_specs=(P("win", None, "sp", None), P("win", "vel", "sp", None)),
        check_vma=False,
    )
```
